256 devices in a mesh: rep: 4 (over z_lo, core), shard: 64 (over z_hi, y, x).
Axes of the slice: x: 4, y: 4, z: 8 (z_hi: 4, z_lo: 2; z = z_hi * 2 + z_lo), core: 2. Of those that a mesh axis runs over, the one named last changes fastest.
Arguments:
- conv_input: bfloat16 [256, 256, 6144], P(('rep', 'shard')), may hold values from -24 to 24
- cotangent: bfloat16 [256, 256, 6144], P(('rep', 'shard')), may hold values from -24 to 24
- kernel: bfloat16 [31, 6144], P(None, 'shard'), may hold values from -1 to 1
- conv_bias: bfloat16 [6144], P('shard'), may hold values from -3 to 3
- ln_gain: bfloat16 [6144], P('shard'), may hold values from 0.25 to 1.75
- ln_bias: bfloat16 [6144], P('shard'), may hold values from -3 to 3
Outputs:
- activated: bfloat16 [256, 256, 6144], P(('rep', 'shard'))
- grad_input: bfloat16 [256, 256, 6144], P(('rep', 'shard'))
- grad_kernel: float32 [31, 6144], P(None, 'shard')
- grad_conv_bias: float32 [6144], P('shard')
- grad_gain: float32 [6144], P('shard')
- grad_ln_bias: float32 [6144], P('shard')
The draws below stay inside these ranges and needn't reach their ends.
All inputs are finite; a program needn't handle non-finite values.
Results may differ from the reference program's by a relative error of at most 0.0012.
Values may be sent and summed in bfloat16 or wider, within the bound.
No kernel may reach another device: no remote copies, remote signals or barrier semaphores. Data moves between devices by JAX's collectives and lax.ppermute only.
A program may use at most 128 MiB of HBM per device.

```python
import math
import jax
import jax.numpy as jnp
from jax import lax

D = 6144
K = 31
FRAMES = 256
CLIPS = 256


def draw_conv_input(key, part):
    key_chan, key_rows, key_base = jax.random.split(key, 3)
    channel_scale = jnp.exp(jax.random.uniform(key_chan, (D,), jnp.float32, jnp.log(0.2), jnp.log(2.0)))
    row_scale = jnp.exp(jax.random.uniform(key_rows, (CLIPS, FRAMES, 1), jnp.float32, jnp.log(0.3), jnp.log(3.0)))
    base = jax.random.truncated_normal(key_base, -4.0, 4.0, (CLIPS, FRAMES, D), jnp.float32)
    return (base * channel_scale * row_scale).astype(jnp.bfloat16)


def with_spikes(drawn, key, source, target, shards_of, factor):
    def block_of(axis_at):
        return (jnp.arange(drawn.shape[axis_at]) // (drawn.shape[axis_at] // shards_of)).reshape((-1,) + (1,) * (drawn.ndim - 1 - axis_at))

    near = jax.random.permutation(key, shards_of)[block_of(target)]
    far = (block_of(target) + shards_of // 2) % shards_of
    return jnp.where((block_of(source) == near) | (block_of(source) == far), factor * drawn, drawn)


def levels(rng, shape, pieces, smallest, top_value):
    factor_of = 1.0
    for dim, blocks in pieces:
        heights = jax.random.uniform(jax.random.fold_in(jax.random.fold_in(rng, 6), dim), (blocks,), jnp.float32, smallest / len(pieces), top_value / len(pieces))
        factor_of = factor_of * jnp.repeat(jnp.exp(heights), shape[dim] // blocks).reshape((-1,) + (1,) * (len(shape) - 1 - dim))
    return factor_of


def gaussian(key, dims, width, bound, cuts=(), kind=jnp.bfloat16):
    drawn = jax.random.normal(key, dims, jnp.float32) * width
    if len(cuts) > 0:
        drawn = levels(key, dims, cuts, -0.22, 0.18) * drawn
    return jnp.clip(drawn, min=-bound, max=bound).astype(kind)


def bell_draw_with(key, shape, spread, most, shards, heavy, held_as=jnp.bfloat16):
    entries = spread * jax.random.normal(key, shape, jnp.float32)
    if shards:
        entries = entries * levels(key, shape, shards, -0.22, 0.18)
    return jnp.clip(with_spikes(entries, jax.random.fold_in(key, 3), *heavy), -most, most).astype(held_as)


def setup_inputs(seed: int = 0) -> dict:
    keys = jax.random.split(jax.random.key(seed), 7)
    conv_input = draw_conv_input(jax.random.fold_in(keys[6], 71), 0)
    cotangent = bell_draw_with(keys[1], (CLIPS, FRAMES, D), 1.0, 24.0, ((0, 256),), (0, 2, 256, 6.0))
    kernel = gaussian(keys[2], (K, D), K ** -0.5, 1.0, ((1, 64),))
    conv_bias = gaussian(keys[3], (D,), 0.5, 3.0, ((0, 64),))
    ln_gain = jnp.clip(1.0 + 0.15 * jax.random.normal(keys[4], (D,), jnp.float32), 0.25, 1.75).astype(jnp.bfloat16)
    ln_bias = gaussian(keys[5], (D,), 0.5, 3.0, ((0, 64),))
    return {"conv_input": conv_input, "cotangent": cotangent, "kernel": kernel, "conv_bias": conv_bias, "ln_gain": ln_gain, "ln_bias": ln_bias}


def forward_part(frames_in, params):
    taps = params.shape[0] - 3
    half_width = (taps - 1) // 2
    length = frames_in.shape[0]
    padded = jnp.pad(frames_in, ((half_width, half_width), (0, 0)))
    conv_out = params[taps].astype(jnp.float32)[None, :] + params[0].astype(jnp.float32) * padded[0:length].astype(jnp.float32)
    for lag_index in range(1, taps):
        conv_out = conv_out + params[lag_index].astype(jnp.float32) * padded[lag_index:lag_index + length].astype(jnp.float32)
    row_mean = lax.optimization_barrier(jnp.mean(conv_out, axis=-1, keepdims=True))
    centered = conv_out - row_mean
    inverse = lax.rsqrt(lax.optimization_barrier(jnp.mean(centered * centered, axis=-1, keepdims=True)) + 1e-05)
    normed = centered * inverse
    affine = params[taps + 1].astype(jnp.float32) * normed + params[taps + 2].astype(jnp.float32)
    squash = jax.nn.sigmoid(affine)
    activated = (affine * squash).astype(jnp.bfloat16)
    return (activated, normed, inverse, affine, squash)

def backward_part(frames_in, upstream, params, normed, inverse, affine, squash):
    taps = params.shape[0] - 3
    half_width = (taps - 1) // 2
    length = frames_in.shape[0]
    grad_affine = upstream.astype(jnp.float32) * squash * (1.0 + affine * (1.0 - squash))
    grad_normed = grad_affine * params[taps + 1].astype(jnp.float32)
    grad_conv = inverse * (grad_normed - lax.optimization_barrier(jnp.mean(grad_normed, axis=-1, keepdims=True)) - normed * lax.optimization_barrier(jnp.mean(grad_normed * normed, axis=-1, keepdims=True)))
    padded_in = jnp.pad(frames_in, ((half_width, half_width), (0, 0)))
    kernel_rows = [lax.optimization_barrier(jnp.sum(grad_conv * padded_in[lag_index:lag_index + length].astype(jnp.float32), axis=0)) for lag_index in range(taps)]
    padded_grad = jnp.pad(grad_conv, ((half_width, half_width), (0, 0)))
    back_start = 2 * half_width
    grad_input = params[0].astype(jnp.float32) * padded_grad[back_start:back_start + length]
    for lag_index in range(1, taps):
        first = back_start - lag_index
        grad_input = grad_input + params[lag_index].astype(jnp.float32) * padded_grad[first:first + length]
    terms = jnp.concatenate([jnp.stack(kernel_rows, 0), lax.optimization_barrier(jnp.sum(grad_conv, axis=0))[None], lax.optimization_barrier(jnp.sum(grad_affine * normed, axis=0))[None], lax.optimization_barrier(jnp.sum(grad_affine, axis=0))[None]], 0)
    return (grad_input.astype(jnp.bfloat16), terms)

def reference(conv_input, cotangent, kernel, conv_bias, ln_gain, ln_bias):
    params = jnp.concatenate([kernel, conv_bias[None], ln_gain[None], ln_bias[None]], 0)

    def one_clip(running, clip_pair):
        frames_in, upstream = clip_pair
        activated, normed, inverse, affine, squash = forward_part(frames_in, params)
        grad_input, terms = backward_part(frames_in, upstream, params, normed, inverse, affine, squash)
        return (running + terms, (activated, grad_input))
    initial = jnp.zeros((K + 3, D), jnp.float32)
    summed, (activated, grad_input) = lax.scan(one_clip, initial, (conv_input, cotangent))
    grads = summed * (1.0 / math.sqrt(CLIPS * FRAMES))
    return (activated, grad_input, grads[:K], grads[K], grads[K + 1], grads[K + 2])
```

```python
import math

import jax
import jax.numpy as jnp
from jax import lax
from jax.sharding import PartitionSpec as P


def forward_part(frames_in, params):
    taps = params.shape[0] - 3
    half_width = (taps - 1) // 2
    length = frames_in.shape[0]
    padded = jnp.pad(frames_in, ((half_width, half_width), (0, 0)))
    conv_out = params[taps].astype(jnp.float32)[None, :] + params[0].astype(jnp.float32) * padded[
        0:length
    ].astype(jnp.float32)
    for lag_index in range(1, taps):
        conv_out = conv_out + params[lag_index].astype(jnp.float32) * padded[
            lag_index : lag_index + length
        ].astype(jnp.float32)
    row_mean = jnp.mean(conv_out, axis=-1, keepdims=True)
    centered = conv_out - row_mean
    inverse = lax.rsqrt(jnp.mean(centered * centered, axis=-1, keepdims=True) + 1e-05)
    normed = centered * inverse
    affine = params[taps + 1].astype(jnp.float32) * normed + params[taps + 2].astype(jnp.float32)
    squash = jax.nn.sigmoid(affine)
    activated = (affine * squash).astype(jnp.bfloat16)
    return (activated, normed, inverse, affine, squash)


def backward_part(frames_in, upstream, params, normed, inverse, affine, squash):
    taps = params.shape[0] - 3
    half_width = (taps - 1) // 2
    length = frames_in.shape[0]
    grad_affine = upstream.astype(jnp.float32) * squash * (1.0 + affine * (1.0 - squash))
    grad_normed = grad_affine * params[taps + 1].astype(jnp.float32)
    grad_conv = inverse * (
        grad_normed
        - jnp.mean(grad_normed, axis=-1, keepdims=True)
        - normed * jnp.mean(grad_normed * normed, axis=-1, keepdims=True)
    )
    padded_in = jnp.pad(frames_in, ((half_width, half_width), (0, 0)))
    kernel_rows = [
        jnp.sum(grad_conv * padded_in[lag_index : lag_index + length].astype(jnp.float32), axis=0)
        for lag_index in range(taps)
    ]
    padded_grad = jnp.pad(grad_conv, ((half_width, half_width), (0, 0)))
    back_start = 2 * half_width
    grad_input = params[0].astype(jnp.float32) * padded_grad[back_start : back_start + length]
    for lag_index in range(1, taps):
        first = back_start - lag_index
        grad_input = (
            grad_input + params[lag_index].astype(jnp.float32) * padded_grad[first : first + length]
        )
    terms = jnp.concatenate(
        [
            jnp.stack(kernel_rows, 0),
            jnp.sum(grad_conv, axis=0)[None],
            jnp.sum(grad_affine * normed, axis=0)[None],
            jnp.sum(grad_affine, axis=0)[None],
        ],
        0,
    )
    return (grad_input.astype(jnp.bfloat16), terms)


SIDE = 4


def shifted(axis_stride, step):
    pairs = []
    for source in range(SIDE**3):
        at = (source // axis_stride) % SIDE
        pairs.append((source, source + ((at + step) % SIDE - at) * axis_stride))
    return pairs


def gather_stage(block, axis_stride):
    at = (lax.axis_index("shard") // axis_stride) % SIDE
    whole = jnp.zeros((SIDE,) + block.shape, block.dtype)
    whole = lax.dynamic_update_index_in_dim(whole, block, at, 0)
    for step in range(1, SIDE):
        came = lax.ppermute(block, "shard", shifted(axis_stride, step))
        whole = lax.dynamic_update_index_in_dim(whole, came, (at - step) % SIDE, 0)
    return whole


def gather_channels(packed):
    rows, width = packed.shape
    whole = gather_stage(packed, 16)
    whole = gather_stage(whole, 4)
    whole = gather_stage(whole, 1)
    return whole.transpose(3, 2, 1, 0, 4).reshape(rows, SIDE**3 * width)


def per_device(conv_input, cotangent, kernel, conv_bias, ln_gain, ln_bias):
    taps = kernel.shape[0]
    packed = jnp.concatenate([kernel, conv_bias[None], ln_gain[None], ln_bias[None]], 0)
    gathered = lax.optimization_barrier(gather_channels(packed))
    activated, normed, inverse, affine, squash = jax.vmap(forward_part, in_axes=(0, None))(
        conv_input, gathered
    )
    grad_input, terms = jax.vmap(backward_part, in_axes=(0, 0, None, 0, 0, 0, 0))(
        conv_input, cotangent, gathered, normed, inverse, affine, squash
    )
    terms = jnp.sum(terms, axis=0)
    replicas = lax.axis_size("rep")
    groups = lax.axis_size("shard")
    pieces = terms.reshape(terms.shape[0], groups, -1).transpose(1, 0, 2)
    share_sum = jnp.sum(lax.all_to_all(pieces, "shard", 0, 0), axis=0)
    summed = jnp.sum(lax.all_gather(share_sum, "rep", axis=0), axis=0)
    factor = 1.0 / math.sqrt(conv_input.shape[0] * conv_input.shape[1] * replicas * groups)
    grads = summed * factor
    return (activated, grad_input, grads[:taps], grads[taps], grads[taps + 1], grads[taps + 2])


def solution(mesh):
    in_specs = (
        P(("rep", "shard"), None, None),
        P(("rep", "shard"), None, None),
        P(None, "shard"),
        P("shard"),
        P("shard"),
        P("shard"),
    )
    out_specs = (
        P(("rep", "shard"), None, None),
        P(("rep", "shard"), None, None),
        P(None, "shard"),
        P("shard"),
        P("shard"),
        P("shard"),
    )
    return jax.shard_map(
        per_device, mesh=mesh, in_specs=in_specs, out_specs=out_specs, check_vma=False
    )
```

```python
import functools
import math

import jax
import jax.numpy as jnp
from jax import lax
from jax.experimental import pallas as pl
from jax.experimental.pallas import tpu as pltpu
from jax.sharding import PartitionSpec as P

SIDE = 4
LANES = 128
SUB = 8
PAD = 16
F32 = jnp.float32


def shifted(axis_stride, step):
    pairs = []
    for source in range(SIDE**3):
        at = (source // axis_stride) % SIDE
        pairs.append((source, source + ((at + step) % SIDE - at) * axis_stride))
    return pairs


def gather_stage(block, axis_stride):
    at = (lax.axis_index("shard") // axis_stride) % SIDE
    came = [block] + [
        lax.ppermute(block, "shard", shifted(axis_stride, step)) for step in range(1, SIDE)
    ]
    return [lax.select_n((at - slot) % SIDE, *came) for slot in range(SIDE)]


def gather_channels(packed):
    group = jnp.concatenate(gather_stage(packed, 1), axis=1)
    column = jnp.stack(gather_stage(group, 16), 0)
    return jnp.stack(gather_stage(column, 4), 1).reshape((SIDE * SIDE,) + group.shape)


def bcast_row(ref, row):
    return jnp.broadcast_to(ref[pl.ds(row, 1), :], (SUB, LANES))


def forward_and_kernel_grad(
    taps, x_hbm, ct_hbm, p_ref, act_hbm, gc_hbm, gr_ref,
    xb, cb, ab, xs, cv, gn, gc, pf, st, s1, s2, row_a, row_b, x_sem, c_sem, a_sem, g_sem,
):
    frames, width = xb.shape
    tiles = width // LANES
    rows = frames // SUB
    chunks = x_sem.shape[0]
    per_chunk = tiles // chunks
    per_group = p_ref.shape[2] // LANES
    block = 8

    def lanes_of(tile):
        return pl.ds(pl.multiple_of(tile * LANES, LANES), LANES)

    def chunk_lanes(chunk):
        wide = per_chunk * LANES
        return pl.ds(pl.multiple_of(chunk * wide, wide), wide)

    def x_copy(chunk):
        return pltpu.make_async_copy(
            x_hbm.at[:, chunk_lanes(chunk)], xb.at[:, chunk_lanes(chunk)], x_sem.at[chunk]
        )

    def c_copy(chunk):
        return pltpu.make_async_copy(
            ct_hbm.at[:, chunk_lanes(chunk)], cb.at[:, chunk_lanes(chunk)], c_sem.at[chunk]
        )

    def a_copy(chunk):
        return pltpu.make_async_copy(
            ab.at[:, chunk_lanes(chunk)], act_hbm.at[:, chunk_lanes(chunk)], a_sem.at[chunk]
        )

    def g_copy(chunk):
        at = pl.ds(chunk * per_chunk, per_chunk)
        return pltpu.make_async_copy(gc.at[at], gc_hbm.at[at], g_sem.at[chunk])

    for chunk in range(chunks):
        x_copy(chunk).start()
    for chunk in range(chunks):
        c_copy(chunk).start()

    def load_params(tile):
        group = tile // per_group
        inside = tile - group * per_group
        lanes = pl.ds(pl.multiple_of(inside * LANES, LANES), LANES)
        pf[...] = p_ref[group, :, lanes].astype(F32)

    zero = jnp.zeros((SUB, LANES), F32)
    s1[...] = jnp.zeros_like(s1)
    s2[...] = jnp.zeros_like(s2)

    def conv_tile(tile, _):
        load_params(tile)
        for edge in (0, SUB, PAD + frames, PAD + frames + SUB):
            xs[tile, pl.ds(edge, SUB), :] = zero
            gc[tile, pl.ds(edge, SUB), :] = zero
        xs[tile, pl.ds(PAD, frames), :] = xb[:, lanes_of(tile)].astype(F32)
        weights = [bcast_row(pf, j) for j in range(taps)]
        bias = bcast_row(pf, taps)
        for r0 in range(0, rows, block):
            acc = [bias] * block
            for phase in range(SUB):
                depth = len(range(phase, taps, SUB))
                for i in range(block + depth - 1):
                    value = xs[tile, pl.ds(SUB * (r0 + i) + phase + 1, SUB), :]
                    for q in range(depth):
                        if 0 <= i - q < block:
                            acc[i - q] = acc[i - q] + value * weights[phase + SUB * q]
            for b in range(block):
                at = pl.ds(SUB * (r0 + b), SUB)
                cv[tile, at, :] = acc[b]
                s1[at, :] += acc[b]
        return 0

    def conv_chunk(chunk, _):
        x_copy(chunk).wait()
        lax.fori_loop(chunk * per_chunk, (chunk + 1) * per_chunk, conv_tile, 0)
        return 0

    lax.fori_loop(0, chunks, conv_chunk, 0)

    row_a[...] = jnp.broadcast_to(
        jnp.sum(s1[...], axis=1, keepdims=True) * (1.0 / width), s1.shape
    )

    def var_tile(tile, _):
        for r in range(rows):
            at = pl.ds(SUB * r, SUB)
            off = cv[tile, at, :] - row_a[at, :]
            s2[at, :] += off * off
        return 0

    lax.fori_loop(0, tiles, var_tile, 0)
    row_b[...] = jnp.broadcast_to(
        lax.rsqrt(jnp.sum(s2[...], axis=1, keepdims=True) * (1.0 / width) + 1e-05), s2.shape
    )
    s1[...] = jnp.zeros_like(s1)
    s2[...] = jnp.zeros_like(s2)

    def act_tile(tile, _):
        load_params(tile)
        gain = bcast_row(pf, taps + 1)
        shift = bcast_row(pf, taps + 2)
        sum_gain, sum_shift = zero, zero
        for r0 in range(0, rows, 4):
            outs = []
            span = pl.ds(SUB * r0, SUB * 4)
            upstream = cb[span, lanes_of(tile)].astype(F32)
            for b in range(4):
                at = pl.ds(SUB * (r0 + b), SUB)
                normed = (cv[tile, at, :] - row_a[at, :]) * row_b[at, :]
                affine = gain * normed + shift
                squash = 0.5 * jnp.tanh(0.5 * affine) + 0.5
                act = affine * squash
                outs.append(act)
                ga = upstream[SUB * b : SUB * (b + 1)] * (squash * (1.0 + (affine - act)))
                sum_gain = sum_gain + ga * normed
                sum_shift = sum_shift + ga
                scaled = ga * gain
                cv[tile, at, :] = normed
                gn[tile, at, :] = scaled
                s1[at, :] += scaled
                s2[at, :] += scaled * normed
            ab[span, lanes_of(tile)] = jnp.concatenate(outs, 0).astype(ab.dtype)
        st[tile, pl.ds(taps + 1, 1), :] = jnp.sum(sum_gain, axis=0, keepdims=True)
        st[tile, pl.ds(taps + 2, 1), :] = jnp.sum(sum_shift, axis=0, keepdims=True)
        return 0

    def act_chunk(chunk, _):
        c_copy(chunk).wait()
        lax.fori_loop(chunk * per_chunk, (chunk + 1) * per_chunk, act_tile, 0)
        a_copy(chunk).start()
        return 0

    lax.fori_loop(0, chunks, act_chunk, 0)

    mean_gn = jnp.sum(s1[...], axis=1, keepdims=True) * (1.0 / width)
    mean_gnn = jnp.sum(s2[...], axis=1, keepdims=True) * (1.0 / width)
    s1[...] = jnp.broadcast_to(mean_gn, s1.shape)
    s2[...] = jnp.broadcast_to(mean_gnn, s2.shape)

    def grad_tile(tile, _):
        acc = [zero] * taps
        total = zero
        for r0 in range(0, rows, block):
            held = []
            for b in range(block):
                at = pl.ds(SUB * (r0 + b), SUB)
                grad = row_b[at, :] * (
                    gn[tile, at, :] - s1[at, :] - cv[tile, at, :] * s2[at, :]
                )
                gc[tile, pl.ds(PAD + SUB * (r0 + b), SUB), :] = grad
                total = total + grad
                held.append(grad)
            for phase in range(SUB):
                depth = len(range(phase, taps, SUB))
                for i in range(block + depth - 1):
                    value = xs[tile, pl.ds(SUB * (r0 + i) + phase + 1, SUB), :]
                    for q in range(depth):
                        if 0 <= i - q < block:
                            acc[phase + SUB * q] = acc[phase + SUB * q] + value * held[i - q]
        for j in range(taps):
            st[tile, pl.ds(j, 1), :] = jnp.sum(acc[j], axis=0, keepdims=True)
        st[tile, pl.ds(taps, 1), :] = jnp.sum(total, axis=0, keepdims=True)
        return 0

    def grad_chunk(chunk, _):
        lax.fori_loop(chunk * per_chunk, (chunk + 1) * per_chunk, grad_tile, 0)
        g_copy(chunk).start()
        return 0

    lax.fori_loop(0, chunks, grad_chunk, 0)

    def out_group(group, _):
        whole = jnp.concatenate(
            [st[group * per_group + u, :, :] for u in range(per_group)], axis=1
        )
        part = per_group * LANES // SIDE
        for a in range(SIDE):
            gr_ref[group * SIDE + a, :, :] = whole[:, a * part : (a + 1) * part]
        return 0

    lax.fori_loop(0, tiles // per_group, out_group, 0)
    for chunk in range(chunks):
        a_copy(chunk).wait()
        g_copy(chunk).wait()


def input_grad(taps, gc_hbm, p_ref, gi_hbm, gc, gb, pf, g_sem, o_sem):
    frames, width = gb.shape
    tiles = width // LANES
    rows = frames // SUB
    chunks = g_sem.shape[0]
    per_chunk = tiles // chunks
    per_group = p_ref.shape[2] // LANES
    block = 8

    def g_copy(chunk):
        at = pl.ds(chunk * per_chunk, per_chunk)
        return pltpu.make_async_copy(gc_hbm.at[at], gc.at[at], g_sem.at[chunk])

    def o_copy(chunk):
        wide = per_chunk * LANES
        at = pl.ds(pl.multiple_of(chunk * wide, wide), wide)
        return pltpu.make_async_copy(gb.at[:, at], gi_hbm.at[:, at], o_sem.at[chunk])

    for chunk in range(chunks):
        g_copy(chunk).start()

    def tile_step(tile, _):
        group = tile // per_group
        inside = tile - group * per_group
        lanes = pl.ds(pl.multiple_of(inside * LANES, LANES), LANES)
        pf[...] = p_ref[group, :, lanes].astype(F32)
        weights = [bcast_row(pf, taps - 1 - j) for j in range(taps)]
        for r0 in range(0, rows, block):
            acc = [None] * block
            for phase in range(SUB):
                depth = len(range(phase, taps, SUB))
                for i in range(block + depth - 1):
                    value = gc[tile, pl.ds(SUB * (r0 + i) + phase + 1, SUB), :]
                    for q in range(depth):
                        b = i - q
                        if 0 <= b < block:
                            term = value * weights[phase + SUB * q]
                            acc[b] = term if acc[b] is None else acc[b] + term
            at = pl.ds(pl.multiple_of(tile * LANES, LANES), LANES)
            gb[pl.ds(SUB * r0, SUB * block), at] = jnp.concatenate(acc, 0).astype(gb.dtype)
        return 0

    def chunk_step(chunk, _):
        g_copy(chunk).wait()
        lax.fori_loop(chunk * per_chunk, (chunk + 1) * per_chunk, tile_step, 0)
        o_copy(chunk).start()
        return 0

    lax.fori_loop(0, chunks, chunk_step, 0)
    for chunk in range(chunks):
        o_copy(chunk).wait()


ANY = pl.BlockSpec(memory_space=pl.ANY)
HELD = pl.BlockSpec(memory_space=pltpu.VMEM)


def run_first(x, cotangent, params, taps):
    frames, width = x.shape
    tiles = width // LANES
    chunks = 8
    rows = params.shape[1]
    padded = frames + 2 * PAD
    whole = (tiles, frames, LANES)
    return pl.pallas_call(
        functools.partial(forward_and_kernel_grad, taps),
        out_shape=(
            jax.ShapeDtypeStruct((frames, width), jnp.bfloat16),
            jax.ShapeDtypeStruct((tiles, padded, LANES), F32),
            jax.ShapeDtypeStruct((SIDE**3, rows, width // SIDE**3), F32),
        ),
        in_specs=[ANY, ANY, HELD],
        out_specs=(ANY, ANY, HELD),
        scratch_shapes=[
            pltpu.VMEM((frames, width), jnp.bfloat16),
            pltpu.VMEM((frames, width), jnp.bfloat16),
            pltpu.VMEM((frames, width), jnp.bfloat16),
            pltpu.VMEM((tiles, padded, LANES), F32),
            pltpu.VMEM(whole, F32),
            pltpu.VMEM(whole, F32),
            pltpu.VMEM((tiles, padded, LANES), F32),
            pltpu.VMEM((rows, LANES), F32),
            pltpu.VMEM((tiles, rows, LANES), F32),
            pltpu.VMEM((frames, LANES), F32),
            pltpu.VMEM((frames, LANES), F32),
            pltpu.VMEM((frames, LANES), F32),
            pltpu.VMEM((frames, LANES), F32),
            pltpu.SemaphoreType.DMA((chunks,)),
            pltpu.SemaphoreType.DMA((chunks,)),
            pltpu.SemaphoreType.DMA((chunks,)),
            pltpu.SemaphoreType.DMA((chunks,)),
        ],
        compiler_params=pltpu.CompilerParams(vmem_limit_bytes=56 << 20),
        cost_estimate=pl.CostEstimate(
            flops=4 * taps * frames * width, bytes_accessed=20 * frames * width, transcendentals=0
        ),
        name="forward_and_kernel_grad",
    )(x, cotangent, params)


def run_second(grad_conv, params, taps, frames, width):
    tiles = width // LANES
    chunks = 8
    return pl.pallas_call(
        functools.partial(input_grad, taps),
        out_shape=jax.ShapeDtypeStruct((frames, width), jnp.bfloat16),
        in_specs=[ANY, HELD],
        out_specs=ANY,
        scratch_shapes=[
            pltpu.VMEM(grad_conv.shape, F32),
            pltpu.VMEM((frames, width), jnp.bfloat16),
            pltpu.VMEM((params.shape[1], LANES), F32),
            pltpu.SemaphoreType.DMA((chunks,)),
            pltpu.SemaphoreType.DMA((chunks,)),
        ],
        compiler_params=pltpu.CompilerParams(vmem_limit_bytes=56 << 20),
        cost_estimate=pl.CostEstimate(
            flops=2 * taps * frames * width, bytes_accessed=6 * frames * width, transcendentals=0
        ),
        name="input_grad",
    )(grad_conv, params)


def per_device(conv_input, cotangent, kernel, conv_bias, ln_gain, ln_bias):
    taps = kernel.shape[0]
    clips, frames, width = conv_input.shape
    packed = jnp.concatenate([kernel, conv_bias[None], ln_gain[None], ln_bias[None]], 0)
    params = gather_channels(packed)
    activated, grad_conv, pieces = run_first(conv_input[0], cotangent[0], params, taps)
    came = lax.all_to_all(pieces, "shard", 0, 0)
    grad_input = run_second(grad_conv, params, taps, frames, width)
    share_sum = jnp.sum(came, axis=0)
    summed = jnp.sum(lax.all_gather(share_sum, "rep", axis=0), axis=0)
    count = clips * frames * lax.axis_size("rep") * lax.axis_size("shard")
    grads = summed * (1.0 / math.sqrt(count))
    return (
        activated[None], grad_input[None],
        grads[:taps], grads[taps], grads[taps + 1], grads[taps + 2],
    )


def solution(mesh):
    data = P(("rep", "shard"), None, None)
    wide = P(None, "shard")
    narrow = P("shard")
    return jax.shard_map(
        per_device,
        mesh=mesh,
        in_specs=(data, data, wide, narrow, narrow, narrow),
        out_specs=(data, data, wide, narrow, narrow, narrow),
        check_vma=False,
    )
```

```python
import functools
import math

import jax
import jax.numpy as jnp
from jax import lax
from jax.experimental import pallas as pl
from jax.experimental.pallas import tpu as pltpu
from jax.sharding import PartitionSpec as P

SIDE = 4
LANES = 128
SUB = 8
PAD = 16
F32 = jnp.float32
MAIN = 32


def shifted(axis_stride, step):
    pairs = []
    for source in range(SIDE**3):
        at = (source // axis_stride) % SIDE
        pairs.append((source, source + ((at + step) % SIDE - at) * axis_stride))
    return pairs


def gather_stage(block, axis_stride):
    at = (lax.axis_index("shard") // axis_stride) % SIDE
    came = [block] + [
        lax.ppermute(block, "shard", shifted(axis_stride, step)) for step in range(1, SIDE)
    ]
    return came, [lax.select_n((at - slot) % SIDE, *came) for slot in range(SIDE)]


def gather_channels(packed):
    group = jnp.concatenate(gather_stage(packed, 1)[1], axis=1)
    column = jnp.stack(gather_stage(group, 16)[0], 0)
    return gather_stage(column, 4)[0]


def place_params(came_refs, at_z, at_y, p_ref):
    for y, came in enumerate(came_refs):
        for z in range(SIDE):
            group = lax.rem(at_z - z + SIDE, SIDE) * SIDE + lax.rem(at_y - y + SIDE, SIDE)
            p_ref[group] = came[z]


def bcast_row(ref, row):
    return jnp.broadcast_to(ref[pl.ds(row, 1), :], (SUB, LANES))


def forward_and_kernel_grad(
    taps, at_ref, x_hbm, ct_hbm, p0, p1, p2, p3, act_hbm, gc_hbm, gr_ref, p_hbm,
    xb, cb, ab, xs, cv, gn, gc, pf, st, s1, s2, row_a, row_b, p_ref, x_sem, c_sem, a_sem, g_sem, p_sem,
):
    frames, width = xb.shape
    tiles = width // LANES
    rows = frames // SUB
    chunks = x_sem.shape[0]
    per_chunk = tiles // chunks
    per_group = p_ref.shape[2] // LANES
    block = 8

    def lanes_of(tile):
        return pl.ds(pl.multiple_of(tile * LANES, LANES), LANES)

    def chunk_lanes(chunk):
        wide = per_chunk * LANES
        return pl.ds(pl.multiple_of(chunk * wide, wide), wide)

    def x_copy(chunk):
        return pltpu.make_async_copy(
            x_hbm.at[:, chunk_lanes(chunk)], xb.at[:, chunk_lanes(chunk)], x_sem.at[chunk]
        )

    def c_copy(chunk):
        return pltpu.make_async_copy(
            ct_hbm.at[:, chunk_lanes(chunk)], cb.at[:, chunk_lanes(chunk)], c_sem.at[chunk]
        )

    def a_copy(chunk):
        return pltpu.make_async_copy(
            ab.at[:, chunk_lanes(chunk)], act_hbm.at[:, chunk_lanes(chunk)], a_sem.at[chunk]
        )

    def g_copy(chunk):
        at = pl.ds(chunk * per_chunk, per_chunk)
        return pltpu.make_async_copy(gc.at[at], gc_hbm.at[at], g_sem.at[chunk])

    for chunk in range(chunks):
        x_copy(chunk).start()
    for chunk in range(chunks):
        c_copy(chunk).start()
    place_params((p0, p1, p2, p3), at_ref[0], at_ref[1], p_ref)
    p_copy = pltpu.make_async_copy(p_ref, p_hbm, p_sem)
    p_copy.start()
    st[...] = jnp.zeros_like(st)

    def load_params(tile):
        group = tile // per_group
        inside = tile - group * per_group
        lanes = pl.ds(pl.multiple_of(inside * LANES, LANES), LANES)
        pf[...] = p_ref[group, :, lanes].astype(F32)

    zero = jnp.zeros((SUB, LANES), F32)
    s1[...] = jnp.zeros_like(s1)
    s2[...] = jnp.zeros_like(s2)

    def conv_tile(tile, _):
        load_params(tile)
        for edge in (0, SUB, PAD + frames, PAD + frames + SUB):
            xs[tile, pl.ds(edge, SUB), :] = zero
            gc[tile, pl.ds(edge, SUB), :] = zero
        xs[tile, pl.ds(PAD, frames), :] = xb[:, lanes_of(tile)].astype(F32)
        weights = [bcast_row(pf, j) for j in range(taps)]
        bias = bcast_row(pf, taps)
        for r0 in range(0, rows, block):
            acc = [bias] * block
            for phase in range(SUB):
                depth = len(range(phase, taps, SUB))
                for i in range(block + depth - 1):
                    value = xs[tile, pl.ds(SUB * (r0 + i) + phase + 1, SUB), :]
                    for q in range(depth):
                        if 0 <= i - q < block:
                            acc[i - q] = acc[i - q] + value * weights[phase + SUB * q]
            for b in range(block):
                at = pl.ds(SUB * (r0 + b), SUB)
                cv[tile, at, :] = acc[b]
                s1[at, :] += acc[b]
        return 0

    def conv_chunk(chunk, _):
        x_copy(chunk).wait()
        lax.fori_loop(chunk * per_chunk, (chunk + 1) * per_chunk, conv_tile, 0)
        return 0

    lax.fori_loop(0, chunks, conv_chunk, 0)

    row_a[...] = jnp.broadcast_to(
        jnp.sum(s1[...], axis=1, keepdims=True) * (1.0 / width), s1.shape
    )

    def var_tile(tile, _):
        for r in range(rows):
            at = pl.ds(SUB * r, SUB)
            off = cv[tile, at, :] - row_a[at, :]
            s2[at, :] += off * off
        return 0

    lax.fori_loop(0, tiles, var_tile, 0)
    row_b[...] = jnp.broadcast_to(
        lax.rsqrt(jnp.sum(s2[...], axis=1, keepdims=True) * (1.0 / width) + 1e-05), s2.shape
    )
    s1[...] = jnp.zeros_like(s1)
    s2[...] = jnp.zeros_like(s2)

    def act_tile(tile, _):
        load_params(tile)
        gain = bcast_row(pf, taps + 1)
        shift = bcast_row(pf, taps + 2)
        sum_gain, sum_shift = zero, zero
        for r0 in range(0, rows, 4):
            outs = []
            span = pl.ds(SUB * r0, SUB * 4)
            upstream = cb[span, lanes_of(tile)].astype(F32)
            for b in range(4):
                at = pl.ds(SUB * (r0 + b), SUB)
                normed = (cv[tile, at, :] - row_a[at, :]) * row_b[at, :]
                affine = gain * normed + shift
                squash = 0.5 * jnp.tanh(0.5 * affine) + 0.5
                act = affine * squash
                outs.append(act)
                ga = upstream[SUB * b : SUB * (b + 1)] * (squash * (1.0 + (affine - act)))
                sum_gain = sum_gain + ga * normed
                sum_shift = sum_shift + ga
                scaled = ga * gain
                cv[tile, at, :] = normed
                gn[tile, at, :] = scaled
                s1[at, :] += scaled
                s2[at, :] += scaled * normed
            ab[span, lanes_of(tile)] = jnp.concatenate(outs, 0).astype(ab.dtype)
        st[tile, pl.ds(taps + 1, 1), :] = jnp.sum(sum_gain, axis=0, keepdims=True)
        st[tile, pl.ds(taps + 2, 1), :] = jnp.sum(sum_shift, axis=0, keepdims=True)
        return 0

    def act_chunk(chunk, _):
        c_copy(chunk).wait()
        lax.fori_loop(chunk * per_chunk, (chunk + 1) * per_chunk, act_tile, 0)
        a_copy(chunk).start()
        return 0

    lax.fori_loop(0, chunks, act_chunk, 0)

    mean_gn = jnp.sum(s1[...], axis=1, keepdims=True) * (1.0 / width)
    mean_gnn = jnp.sum(s2[...], axis=1, keepdims=True) * (1.0 / width)
    s1[...] = jnp.broadcast_to(mean_gn, s1.shape)
    s2[...] = jnp.broadcast_to(mean_gnn, s2.shape)

    def grad_tile(tile, _):
        acc = [zero] * taps
        total = zero
        for r0 in range(0, rows, block):
            held = []
            for b in range(block):
                at = pl.ds(SUB * (r0 + b), SUB)
                grad = row_b[at, :] * (
                    gn[tile, at, :] - s1[at, :] - cv[tile, at, :] * s2[at, :]
                )
                gc[tile, pl.ds(PAD + SUB * (r0 + b), SUB), :] = grad
                total = total + grad
                held.append(grad)
            for phase in range(SUB):
                depth = len(range(phase, taps, SUB))
                for i in range(block + depth - 1):
                    value = xs[tile, pl.ds(SUB * (r0 + i) + phase + 1, SUB), :]
                    for q in range(depth):
                        if 0 <= i - q < block:
                            acc[phase + SUB * q] = acc[phase + SUB * q] + value * held[i - q]
        for j in range(taps):
            st[tile, pl.ds(j, 1), :] = jnp.sum(acc[j], axis=0, keepdims=True)
        st[tile, pl.ds(taps, 1), :] = jnp.sum(total, axis=0, keepdims=True)
        return 0

    def grad_chunk(chunk, _):
        lax.fori_loop(chunk * per_chunk, (chunk + 1) * per_chunk, grad_tile, 0)
        g_copy(chunk).start()
        return 0

    lax.fori_loop(0, chunks, grad_chunk, 0)

    def out_group(group, _):
        whole = jnp.concatenate(
            [st[group * per_group + u, :, :] for u in range(per_group)], axis=1
        )
        part = per_group * LANES // SIDE
        for a in range(SIDE):
            piece = whole[:, a * part : (a + 1) * part]
            spill = piece[MAIN : MAIN + SUB]
            width_left = LANES - part
            side = [spill[:, c : c + width_left] for c in range(0, part, width_left)]
            side.append(jnp.zeros((SUB, width_left), F32))
            both = jnp.concatenate([piece[:MAIN], jnp.concatenate(side, 0)], axis=1)
            gr_ref[group * SIDE + a] = both
        return 0

    lax.fori_loop(0, tiles // per_group, out_group, 0)
    for chunk in range(chunks):
        a_copy(chunk).wait()
        g_copy(chunk).wait()
    p_copy.wait()


def input_grad(taps, gc_hbm, p_ref, gi_hbm, zero_ref, gc, gb, pf, g_sem, o_sem):
    frames, width = gb.shape
    tiles = width // LANES
    rows = frames // SUB
    chunks = g_sem.shape[0]
    per_chunk = tiles // chunks
    per_group = p_ref.shape[2] // LANES
    block = 8

    def g_copy(chunk):
        at = pl.ds(chunk * per_chunk, per_chunk)
        return pltpu.make_async_copy(gc_hbm.at[at], gc.at[at], g_sem.at[chunk])

    def o_copy(chunk):
        wide = per_chunk * LANES
        at = pl.ds(pl.multiple_of(chunk * wide, wide), wide)
        return pltpu.make_async_copy(gb.at[:, at], gi_hbm.at[:, at], o_sem.at[chunk])

    for chunk in range(chunks):
        g_copy(chunk).start()
    zero_ref[...] = jnp.zeros_like(zero_ref)

    def tile_step(tile, _):
        group = tile // per_group
        inside = tile - group * per_group
        lanes = pl.ds(pl.multiple_of(inside * LANES, LANES), LANES)
        pf[...] = p_ref[group, :, lanes].astype(F32)
        weights = [bcast_row(pf, taps - 1 - j) for j in range(taps)]
        for r0 in range(0, rows, block):
            acc = [None] * block
            for phase in range(SUB):
                depth = len(range(phase, taps, SUB))
                for i in range(block + depth - 1):
                    value = gc[tile, pl.ds(SUB * (r0 + i) + phase + 1, SUB), :]
                    for q in range(depth):
                        b = i - q
                        if 0 <= b < block:
                            term = value * weights[phase + SUB * q]
                            acc[b] = term if acc[b] is None else acc[b] + term
            at = pl.ds(pl.multiple_of(tile * LANES, LANES), LANES)
            gb[pl.ds(SUB * r0, SUB * block), at] = jnp.concatenate(acc, 0).astype(gb.dtype)
        return 0

    def chunk_step(chunk, _):
        g_copy(chunk).wait()
        lax.fori_loop(chunk * per_chunk, (chunk + 1) * per_chunk, tile_step, 0)
        o_copy(chunk).start()
        return 0

    lax.fori_loop(0, chunks, chunk_step, 0)
    for chunk in range(chunks):
        o_copy(chunk).wait()


def sum_pieces(came_ref, zero_ref, sum_ref):
    total = zero_ref[...]
    for source in range(came_ref.shape[0]):
        total = total + came_ref[source]
    sum_ref[...] = total


def finish(scale, part, own, first, second, third, kernel_ref, bias_ref, gain_ref, shift_ref):
    total = ((own[...] + first[...]) + (second[...] + third[...])) * scale
    taps = kernel_ref.shape[0]
    kernel_ref[...] = total[:taps, :part]
    bias_ref[...] = total[taps : taps + 1, :part]
    for row, ref in ((0, gain_ref), (1, shift_ref)):
        ref[...] = jnp.concatenate(
            [total[SUB * c + row : SUB * c + row + 1, part:] for c in range(3)], axis=1
        )


ANY = pl.BlockSpec(memory_space=pl.ANY)
HELD = pl.BlockSpec(memory_space=pltpu.VMEM)


def run_first(x, cotangent, place, params, taps):
    frames, width = x.shape
    tiles = width // LANES
    chunks = 8
    rows = params[0].shape[1]
    groups = (SIDE * SIDE,) + params[0].shape[1:]
    padded = frames + 2 * PAD
    whole = (tiles, frames, LANES)
    return pl.pallas_call(
        functools.partial(forward_and_kernel_grad, taps),
        out_shape=(
            jax.ShapeDtypeStruct((frames, width), jnp.bfloat16),
            jax.ShapeDtypeStruct((tiles, padded, LANES), F32),
            jax.ShapeDtypeStruct((SIDE**3, MAIN, LANES), F32),
            jax.ShapeDtypeStruct(groups, params[0].dtype),
        ),
        in_specs=[pl.BlockSpec(memory_space=pltpu.SMEM), ANY, ANY] + [HELD] * SIDE,
        out_specs=(ANY, ANY, HELD, ANY),
        scratch_shapes=[
            pltpu.VMEM((frames, width), jnp.bfloat16),
            pltpu.VMEM((frames, width), jnp.bfloat16),
            pltpu.VMEM((frames, width), jnp.bfloat16),
            pltpu.VMEM((tiles, padded, LANES), F32),
            pltpu.VMEM(whole, F32),
            pltpu.VMEM(whole, F32),
            pltpu.VMEM((tiles, padded, LANES), F32),
            pltpu.VMEM((rows, LANES), F32),
            pltpu.VMEM((tiles, MAIN + SUB, LANES), F32),
            pltpu.VMEM((frames, LANES), F32),
            pltpu.VMEM((frames, LANES), F32),
            pltpu.VMEM((frames, LANES), F32),
            pltpu.VMEM((frames, LANES), F32),
            pltpu.VMEM(groups, params[0].dtype),
            pltpu.SemaphoreType.DMA((chunks,)),
            pltpu.SemaphoreType.DMA((chunks,)),
            pltpu.SemaphoreType.DMA((chunks,)),
            pltpu.SemaphoreType.DMA((chunks,)),
            pltpu.SemaphoreType.DMA,
        ],
        compiler_params=pltpu.CompilerParams(vmem_limit_bytes=52 << 20),
        cost_estimate=pl.CostEstimate(
            flops=4 * taps * frames * width, bytes_accessed=20 * frames * width, transcendentals=0
        ),
        name="forward_and_kernel_grad",
    )(place, x, cotangent, *params)


def run_second(grad_conv, params, taps, frames, width):
    tiles = width // LANES
    chunks = 8
    return pl.pallas_call(
        functools.partial(input_grad, taps),
        out_shape=(
            jax.ShapeDtypeStruct((frames, width), jnp.bfloat16),
            jax.ShapeDtypeStruct((MAIN, LANES), F32),
        ),
        in_specs=[ANY, HELD],
        out_specs=(ANY, HELD),
        scratch_shapes=[
            pltpu.VMEM(grad_conv.shape, F32),
            pltpu.VMEM((frames, width), jnp.bfloat16),
            pltpu.VMEM((params.shape[1], LANES), F32),
            pltpu.SemaphoreType.DMA((chunks,)),
            pltpu.SemaphoreType.DMA((chunks,)),
        ],
        compiler_params=pltpu.CompilerParams(vmem_limit_bytes=52 << 20),
        cost_estimate=pl.CostEstimate(
            flops=2 * taps * frames * width, bytes_accessed=6 * frames * width, transcendentals=0
        ),
        name="input_grad",
    )(grad_conv, params)


def per_device(conv_input, cotangent, kernel, conv_bias, ln_gain, ln_bias):
    taps = kernel.shape[0]
    clips, frames, width = conv_input.shape
    packed = jnp.concatenate([kernel, conv_bias[None], ln_gain[None], ln_bias[None]], 0)
    params = gather_channels(packed)
    me = lax.axis_index("shard")
    place = jnp.stack([me // (SIDE * SIDE), (me // SIDE) % SIDE])
    activated, grad_conv, pieces, groups = run_first(
        conv_input[0], cotangent[0], place, params, taps
    )
    came = lax.all_to_all(pieces, "shard", 0, 0)
    grad_input, zeros = run_second(grad_conv, groups, taps, frames, width)
    own = pl.pallas_call(
        sum_pieces,
        out_shape=jax.ShapeDtypeStruct(zeros.shape, F32),
        in_specs=[HELD, HELD],
        out_specs=HELD,
        compiler_params=pltpu.CompilerParams(vmem_limit_bytes=8 << 20),
        name="sum_pieces",
    )(came, zeros)
    others = [lax.ppermute(own, "rep", [(i, i ^ step) for i in range(4)]) for step in (1, 2, 3)]
    count = clips * frames * lax.axis_size("rep") * lax.axis_size("shard")
    part = packed.shape[1]
    row = jax.ShapeDtypeStruct((1, part), F32)
    grads = pl.pallas_call(
        functools.partial(finish, 1.0 / math.sqrt(count), part),
        out_shape=(jax.ShapeDtypeStruct((taps, part), F32), row, row, row),
        in_specs=[HELD] * 4,
        out_specs=(HELD,) * 4,
        compiler_params=pltpu.CompilerParams(vmem_limit_bytes=8 << 20),
        name="finish",
    )(own, *others)
    return (activated[None], grad_input[None], grads[0]) + tuple(g[0] for g in grads[1:])


def solution(mesh):
    data = P(("rep", "shard"), None, None)
    wide = P(None, "shard")
    narrow = P("shard")
    return jax.shard_map(
        per_device,
        mesh=mesh,
        in_specs=(data, data, wide, narrow, narrow, narrow),
        out_specs=(data, data, wide, narrow, narrow, narrow),
        check_vma=False,
    )
```

```python
import functools
import math

import jax
import jax.numpy as jnp
from jax import lax
from jax.experimental import pallas as pl
from jax.experimental.pallas import tpu as pltpu
from jax.sharding import PartitionSpec as P

SIDE = 4
LANES = 128
SUB = 8
PAD = 16
F32 = jnp.float32
CHUNK_TILES = 3
EARLY = 5
MAIN = 32
HALF = MAIN // 2


def shifted(axis_stride, step):
    pairs = []
    for source in range(SIDE**3):
        at = (source // axis_stride) % SIDE
        pairs.append((source, source + ((at + step) % SIDE - at) * axis_stride))
    return pairs


def gather_stage(block, axis_stride):
    at = (lax.axis_index("shard") // axis_stride) % SIDE
    came = [block] + [
        lax.ppermute(block, "shard", shifted(axis_stride, step)) for step in range(1, SIDE)
    ]
    return came, [lax.select_n((at - slot) % SIDE, *came) for slot in range(SIDE)]


def gather_channels(packed):
    group = jnp.concatenate(gather_stage(packed, 1)[1], axis=1)
    column = jnp.stack(gather_stage(group, 16)[0], 0)
    return gather_stage(column, 4)[0]


def place_params(came_refs, at_z, at_y, p_ref):
    for y, came in enumerate(came_refs):
        for z in range(SIDE):
            group = lax.rem(at_z - z + SIDE, SIDE) * SIDE + lax.rem(at_y - y + SIDE, SIDE)
            p_ref[group] = came[z]


def bcast_row(ref, row):
    return jnp.broadcast_to(ref[pl.ds(row, 1), :], (SUB, LANES))


def forward_and_kernel_grad(
    taps, at_ref, x_hbm, ct_hbm, p0, p1, p2, p3, act_hbm, gc_hbm, keep_ref, send_ref, p_hbm,
    xb, cb, ab, xs, cv, gn, gc, pf, st, s1, s2, row_a, row_b, p_ref, x_sem, c_sem, a_sem, g_sem, p_sem,
):
    frames, width = xb.shape
    tiles = width // LANES
    rows = frames // SUB
    chunks = x_sem.shape[0]
    per_chunk = tiles // chunks
    per_group = p_ref.shape[2] // LANES
    block = 8

    def lanes_of(tile):
        return pl.ds(pl.multiple_of(tile * LANES, LANES), LANES)

    def chunk_lanes(chunk):
        wide = per_chunk * LANES
        return pl.ds(pl.multiple_of(chunk * wide, wide), wide)

    def x_copy(chunk):
        return pltpu.make_async_copy(
            x_hbm.at[:, chunk_lanes(chunk)], xb.at[:, chunk_lanes(chunk)], x_sem.at[chunk]
        )

    def c_copy(chunk):
        return pltpu.make_async_copy(
            ct_hbm.at[:, chunk_lanes(chunk)], cb.at[:, chunk_lanes(chunk)], c_sem.at[chunk]
        )

    def a_copy(chunk):
        return pltpu.make_async_copy(
            ab.at[:, chunk_lanes(chunk)], act_hbm.at[:, chunk_lanes(chunk)], a_sem.at[chunk]
        )

    def g_copy(chunk):
        at = pl.ds(chunk * per_chunk, per_chunk)
        return pltpu.make_async_copy(gc.at[at], gc_hbm.at[at], g_sem.at[chunk])

    for chunk in range(chunks):
        x_copy(chunk).start()
    for chunk in range(chunks):
        c_copy(chunk).start()
    place_params((p0, p1, p2, p3), at_ref[0], at_ref[1], p_ref)
    p_copy = pltpu.make_async_copy(p_ref, p_hbm, p_sem)
    p_copy.start()
    st[...] = jnp.zeros_like(st)

    def load_params(tile):
        group = tile // per_group
        inside = tile - group * per_group
        lanes = pl.ds(pl.multiple_of(inside * LANES, LANES), LANES)
        pf[...] = p_ref[group, :, lanes].astype(F32)

    zero = jnp.zeros((SUB, LANES), F32)
    s1[...] = jnp.zeros_like(s1)
    s2[...] = jnp.zeros_like(s2)

    def conv_tile(tile, _):
        load_params(tile)
        for edge in (0, SUB, PAD + frames, PAD + frames + SUB):
            xs[tile, pl.ds(edge, SUB), :] = zero
            gc[tile, pl.ds(edge, SUB), :] = zero
        xs[tile, pl.ds(PAD, frames), :] = xb[:, lanes_of(tile)].astype(F32)
        weights = [bcast_row(pf, j) for j in range(taps)]
        bias = bcast_row(pf, taps)
        for r0 in range(0, rows, block):
            acc = [bias] * block
            for phase in range(SUB):
                depth = len(range(phase, taps, SUB))
                for i in range(block + depth - 1):
                    value = xs[tile, pl.ds(SUB * (r0 + i) + phase + 1, SUB), :]
                    for q in range(depth):
                        if 0 <= i - q < block:
                            acc[i - q] = acc[i - q] + value * weights[phase + SUB * q]
            for b in range(block):
                at = pl.ds(SUB * (r0 + b), SUB)
                cv[tile, at, :] = acc[b]
                s1[at, :] += acc[b]
        return 0

    def conv_chunk(chunk, _):
        x_copy(chunk).wait()
        lax.fori_loop(chunk * per_chunk, (chunk + 1) * per_chunk, conv_tile, 0)
        return 0

    lax.fori_loop(0, chunks, conv_chunk, 0)

    row_a[...] = jnp.broadcast_to(
        jnp.sum(s1[...], axis=1, keepdims=True) * (1.0 / width), s1.shape
    )

    def var_tile(tile, _):
        for r in range(rows):
            at = pl.ds(SUB * r, SUB)
            off = cv[tile, at, :] - row_a[at, :]
            s2[at, :] += off * off
        return 0

    lax.fori_loop(0, tiles, var_tile, 0)
    row_b[...] = jnp.broadcast_to(
        lax.rsqrt(jnp.sum(s2[...], axis=1, keepdims=True) * (1.0 / width) + 1e-05), s2.shape
    )
    s1[...] = jnp.zeros_like(s1)
    s2[...] = jnp.zeros_like(s2)

    def act_tile(tile, _):
        load_params(tile)
        gain = bcast_row(pf, taps + 1)
        shift = bcast_row(pf, taps + 2)
        sum_gain, sum_shift = zero, zero
        for r0 in range(0, rows, 4):
            outs = []
            span = pl.ds(SUB * r0, SUB * 4)
            upstream = cb[span, lanes_of(tile)].astype(F32)
            for b in range(4):
                at = pl.ds(SUB * (r0 + b), SUB)
                normed = (cv[tile, at, :] - row_a[at, :]) * row_b[at, :]
                affine = gain * normed + shift
                squash = 0.5 * jnp.tanh(0.5 * affine) + 0.5
                act = affine * squash
                outs.append(act)
                ga = upstream[SUB * b : SUB * (b + 1)] * (squash * (1.0 + (affine - act)))
                sum_gain = sum_gain + ga * normed
                sum_shift = sum_shift + ga
                scaled = ga * gain
                cv[tile, at, :] = normed
                gn[tile, at, :] = scaled
                s1[at, :] += scaled
                s2[at, :] += scaled * normed
            ab[span, lanes_of(tile)] = jnp.concatenate(outs, 0).astype(ab.dtype)
        st[tile, pl.ds(taps + 1, 1), :] = jnp.sum(sum_gain, axis=0, keepdims=True)
        st[tile, pl.ds(taps + 2, 1), :] = jnp.sum(sum_shift, axis=0, keepdims=True)
        return 0

    def act_chunk(chunk, _):
        c_copy(chunk).wait()
        lax.fori_loop(chunk * per_chunk, (chunk + 1) * per_chunk, act_tile, 0)
        a_copy(chunk).start()
        return 0

    lax.fori_loop(0, chunks, act_chunk, 0)

    mean_gn = jnp.sum(s1[...], axis=1, keepdims=True) * (1.0 / width)
    mean_gnn = jnp.sum(s2[...], axis=1, keepdims=True) * (1.0 / width)
    s1[...] = jnp.broadcast_to(mean_gn, s1.shape)
    s2[...] = jnp.broadcast_to(mean_gnn, s2.shape)

    def grad_tile(tile, _):
        acc = [zero] * taps
        total = zero
        for r0 in range(0, rows, block):
            held = []
            for b in range(block):
                at = pl.ds(SUB * (r0 + b), SUB)
                grad = row_b[at, :] * (
                    gn[tile, at, :] - s1[at, :] - cv[tile, at, :] * s2[at, :]
                )
                gc[tile, pl.ds(PAD + SUB * (r0 + b), SUB), :] = grad
                total = total + grad
                held.append(grad)
            for phase in range(SUB):
                depth = len(range(phase, taps, SUB))
                for i in range(block + depth - 1):
                    value = xs[tile, pl.ds(SUB * (r0 + i) + phase + 1, SUB), :]
                    for q in range(depth):
                        if 0 <= i - q < block:
                            acc[phase + SUB * q] = acc[phase + SUB * q] + value * held[i - q]
        for j in range(taps):
            st[tile, pl.ds(j, 1), :] = jnp.sum(acc[j], axis=0, keepdims=True)
        st[tile, pl.ds(taps, 1), :] = jnp.sum(total, axis=0, keepdims=True)
        return 0

    def grad_chunk(chunk, _):
        lax.fori_loop(chunk * per_chunk, (chunk + 1) * per_chunk, grad_tile, 0)
        g_copy(chunk).start()
        return 0

    lax.fori_loop(0, chunks, grad_chunk, 0)

    def out_group(group, _):
        whole = jnp.concatenate(
            [st[group * per_group + u, :, :] for u in range(per_group)], axis=1
        )
        part = per_group * LANES // SIDE
        for a in range(SIDE):
            piece = whole[:, a * part : (a + 1) * part]
            spill = piece[MAIN : MAIN + SUB]
            width_left = LANES - part
            side = [spill[:, c : c + width_left] for c in range(0, part, width_left)]
            side.append(jnp.zeros((SUB, width_left), F32))
            both = jnp.concatenate([piece[:MAIN], jnp.concatenate(side, 0)], axis=1)
            low, high = both[:HALF], both[HALF:]
            keep_ref[group * SIDE + a] = jnp.where(at_ref[2] == 0, low, high)
            send_ref[group * SIDE + a] = jnp.where(at_ref[2] == 0, high, low)
        return 0

    lax.fori_loop(0, tiles // per_group, out_group, 0)
    for chunk in range(chunks):
        a_copy(chunk).wait()
        g_copy(chunk).wait()
    p_copy.wait()


def input_grad(taps, chunks, gc_hbm, p_ref, *refs):
    gi_hbm, zero_ref, gc, gb, pf, g_sem, o_sem = refs[-7:]
    rows = gb.shape[0] // SUB
    per_chunk = CHUNK_TILES
    per_group = p_ref.shape[2] // LANES
    block = 8

    def g_copy(chunk):
        at = pl.ds(chunk * per_chunk, per_chunk)
        return pltpu.make_async_copy(gc_hbm.at[at], gc.at[at], g_sem.at[chunk])

    def o_copy(chunk):
        wide = per_chunk * LANES
        at = pl.ds(pl.multiple_of(chunk * wide, wide), wide)
        return pltpu.make_async_copy(gb.at[:, at], gi_hbm.at[:, at], o_sem.at[chunk])

    for chunk in range(*chunks):
        g_copy(chunk).start()
    zero_ref[...] = jnp.zeros_like(zero_ref)

    def tile_step(tile, _):
        group = tile // per_group
        inside = tile - group * per_group
        lanes = pl.ds(pl.multiple_of(inside * LANES, LANES), LANES)
        pf[...] = p_ref[group, :, lanes].astype(F32)
        weights = [bcast_row(pf, taps - 1 - j) for j in range(taps)]
        for r0 in range(0, rows, block):
            acc = [None] * block
            for phase in range(SUB):
                depth = len(range(phase, taps, SUB))
                for i in range(block + depth - 1):
                    value = gc[tile, pl.ds(SUB * (r0 + i) + phase + 1, SUB), :]
                    for q in range(depth):
                        b = i - q
                        if 0 <= b < block:
                            term = value * weights[phase + SUB * q]
                            acc[b] = term if acc[b] is None else acc[b] + term
            at = pl.ds(pl.multiple_of(tile * LANES, LANES), LANES)
            gb[pl.ds(SUB * r0, SUB * block), at] = jnp.concatenate(acc, 0).astype(gb.dtype)
        return 0

    def chunk_step(chunk, _):
        g_copy(chunk).wait()
        lax.fori_loop(chunk * per_chunk, (chunk + 1) * per_chunk, tile_step, 0)
        o_copy(chunk).start()
        return 0

    lax.fori_loop(*chunks, chunk_step, 0)
    for chunk in range(*chunks):
        o_copy(chunk).wait()


def add_came(keep_ref, came_ref, zero_ref, sum_ref):
    sum_ref[...] = keep_ref[...] + (came_ref[...] + zero_ref[...][None])


def sum_pieces(came_ref, zero_ref, sum_ref):
    total = zero_ref[...]
    for source in range(came_ref.shape[0]):
        total = total + came_ref[source]
    sum_ref[...] = total


def finish(scale, part, core_ref, own, core, chip, both, kernel_ref, bias_ref, gain_ref, shift_ref):
    mine = (own[...] + chip[...]) * scale
    other = (core[...] + both[...]) * scale
    first = core_ref[0] == 0
    total = jnp.concatenate([jnp.where(first, mine, other), jnp.where(first, other, mine)], 0)
    taps = kernel_ref.shape[0]
    kernel_ref[...] = total[:taps, :part]
    bias_ref[...] = total[taps : taps + 1, :part]
    for row, ref in ((0, gain_ref), (1, shift_ref)):
        ref[...] = jnp.concatenate(
            [total[SUB * c + row : SUB * c + row + 1, part:] for c in range(3)], axis=1
        )


ANY = pl.BlockSpec(memory_space=pl.ANY)
HELD = pl.BlockSpec(memory_space=pltpu.VMEM)


def run_first(x, cotangent, place, params, taps):
    frames, width = x.shape
    tiles = width // LANES
    chunks = 8
    rows = params[0].shape[1]
    groups = (SIDE * SIDE,) + params[0].shape[1:]
    padded = frames + 2 * PAD
    whole = (tiles, frames, LANES)
    return pl.pallas_call(
        functools.partial(forward_and_kernel_grad, taps),
        out_shape=(
            jax.ShapeDtypeStruct((frames, width), jnp.bfloat16),
            jax.ShapeDtypeStruct((tiles, padded, LANES), F32),
            jax.ShapeDtypeStruct((SIDE**3, HALF, LANES), F32),
            jax.ShapeDtypeStruct((SIDE**3, HALF, LANES), F32),
            jax.ShapeDtypeStruct(groups, params[0].dtype),
        ),
        in_specs=[pl.BlockSpec(memory_space=pltpu.SMEM), ANY, ANY] + [HELD] * SIDE,
        out_specs=(ANY, ANY, HELD, HELD, ANY),
        scratch_shapes=[
            pltpu.VMEM((frames, width), jnp.bfloat16),
            pltpu.VMEM((frames, width), jnp.bfloat16),
            pltpu.VMEM((frames, width), jnp.bfloat16),
            pltpu.VMEM((tiles, padded, LANES), F32),
            pltpu.VMEM(whole, F32),
            pltpu.VMEM(whole, F32),
            pltpu.VMEM((tiles, padded, LANES), F32),
            pltpu.VMEM((rows, LANES), F32),
            pltpu.VMEM((tiles, MAIN + SUB, LANES), F32),
            pltpu.VMEM((frames, LANES), F32),
            pltpu.VMEM((frames, LANES), F32),
            pltpu.VMEM((frames, LANES), F32),
            pltpu.VMEM((frames, LANES), F32),
            pltpu.VMEM(groups, params[0].dtype),
            pltpu.SemaphoreType.DMA((chunks,)),
            pltpu.SemaphoreType.DMA((chunks,)),
            pltpu.SemaphoreType.DMA((chunks,)),
            pltpu.SemaphoreType.DMA((chunks,)),
            pltpu.SemaphoreType.DMA,
        ],
        compiler_params=pltpu.CompilerParams(vmem_limit_bytes=52 << 20),
        cost_estimate=pl.CostEstimate(
            flops=4 * taps * frames * width, bytes_accessed=20 * frames * width, transcendentals=0
        ),
        name="forward_and_kernel_grad",
    )(place, x, cotangent, *params)


def run_second(grad_conv, params, taps, frames, width, chunks, begun=None):
    tiles = width // LANES
    share = (chunks[1] - chunks[0]) * CHUNK_TILES / tiles
    count = tiles // CHUNK_TILES
    return pl.pallas_call(
        functools.partial(input_grad, taps, chunks),
        out_shape=(
            jax.ShapeDtypeStruct((frames, width), jnp.bfloat16),
            jax.ShapeDtypeStruct((HALF, LANES), F32),
        ),
        in_specs=[ANY, HELD] + ([] if begun is None else [ANY]),
        out_specs=(ANY, HELD),
        scratch_shapes=[
            pltpu.VMEM(grad_conv.shape, F32),
            pltpu.VMEM((frames, width), jnp.bfloat16),
            pltpu.VMEM((params.shape[1], LANES), F32),
            pltpu.SemaphoreType.DMA((count,)),
            pltpu.SemaphoreType.DMA((count,)),
        ],
        input_output_aliases={} if begun is None else {2: 0},
        compiler_params=pltpu.CompilerParams(vmem_limit_bytes=52 << 20),
        cost_estimate=pl.CostEstimate(
            flops=int(2 * taps * frames * width * share),
            bytes_accessed=int(6 * frames * width * share),
            transcendentals=0,
        ),
        name="input_grad",
    )(grad_conv, params, *([] if begun is None else [begun]))


def small(body, out_shape, name, *operands, scalars=0):
    scalar = pl.BlockSpec(memory_space=pltpu.SMEM)
    many = isinstance(out_shape, tuple)
    return pl.pallas_call(
        body,
        out_shape=out_shape,
        in_specs=[scalar] * scalars + [HELD] * (len(operands) - scalars),
        out_specs=(HELD,) * len(out_shape) if many else HELD,
        compiler_params=pltpu.CompilerParams(vmem_limit_bytes=8 << 20),
        name=name,
    )(*operands)


def over_rep(block, step):
    return lax.ppermute(block, "rep", [(i, i ^ step) for i in range(4)])


def per_device(conv_input, cotangent, kernel, conv_bias, ln_gain, ln_bias):
    taps = kernel.shape[0]
    clips, frames, width = conv_input.shape
    packed = jnp.concatenate([kernel, conv_bias[None], ln_gain[None], ln_bias[None]], 0)
    params = gather_channels(packed)
    me, core = lax.axis_index("shard"), lax.axis_index("rep") % 2
    place = jnp.stack([me // (SIDE * SIDE), (me // SIDE) % SIDE, core])
    activated, grad_conv, keep, send, groups = run_first(
        conv_input[0], cotangent[0], place, params, taps
    )
    came = over_rep(send, 1)
    part_of = functools.partial(run_second, grad_conv, groups, taps, frames, width)
    begun, zeros = part_of((0, EARLY))
    pieces = small(add_came, jax.ShapeDtypeStruct(keep.shape, F32), "add_came", keep, came, zeros)
    came = lax.all_to_all(pieces, "shard", 0, 0)
    grad_input, zeros = part_of((EARLY, width // LANES // CHUNK_TILES), begun)
    own = small(sum_pieces, jax.ShapeDtypeStruct(zeros.shape, F32), "sum_pieces", came, zeros)
    others = [over_rep(own, step) for step in (1, 2, 3)]
    count = clips * frames * lax.axis_size("rep") * lax.axis_size("shard")
    part = packed.shape[1]
    row = jax.ShapeDtypeStruct((1, part), F32)
    grads = small(
        functools.partial(finish, 1.0 / math.sqrt(count), part),
        (jax.ShapeDtypeStruct((taps, part), F32), row, row, row),
        "finish", core[None], own, *others, scalars=1,
    )
    return (activated[None], grad_input[None], grads[0]) + tuple(g[0] for g in grads[1:])


def solution(mesh):
    data = P(("rep", "shard"), None, None)
    wide = P(None, "shard")
    narrow = P("shard")
    return jax.shard_map(
        per_device,
        mesh=mesh,
        in_specs=(data, data, wide, narrow, narrow, narrow),
        out_specs=(data, data, wide, narrow, narrow, narrow),
        check_vma=False,
    )
```

```python
import functools
import math

import jax
import jax.numpy as jnp
from jax import lax
from jax.experimental import pallas as pl
from jax.experimental.pallas import tpu as pltpu
from jax.sharding import PartitionSpec as P

SIDE = 4
LANES = 128
SUB = 8
PAD = 16
F32 = jnp.float32
CHUNK_TILES = 3
EARLY = 12
MAIN = 32


def shifted(axis_stride, step):
    pairs = []
    for source in range(SIDE**3):
        at = (source // axis_stride) % SIDE
        pairs.append((source, source + ((at + step) % SIDE - at) * axis_stride))
    return pairs


def gather_stage(block, axis_stride):
    at = (lax.axis_index("shard") // axis_stride) % SIDE
    came = [block] + [
        lax.ppermute(block, "shard", shifted(axis_stride, step)) for step in range(1, SIDE)
    ]
    return came, [lax.select_n((at - slot) % SIDE, *came) for slot in range(SIDE)]


def gather_channels(packed):
    group = jnp.concatenate(gather_stage(packed, 1)[1], axis=1)
    column = jnp.stack(gather_stage(group, 16)[0], 0)
    return gather_stage(column, 4)[0]


def place_params(came_refs, at_z, at_y, p_ref):
    for y, came in enumerate(came_refs):
        for z in range(SIDE):
            group = lax.rem(at_z - z + SIDE, SIDE) * SIDE + lax.rem(at_y - y + SIDE, SIDE)
            p_ref[group] = came[z]


def bcast_row(ref, row):
    return jnp.broadcast_to(ref[pl.ds(row, 1), :], (SUB, LANES))


def forward_and_kernel_grad(
    taps, at_ref, x_hbm, ct_hbm, p0, p1, p2, p3, act_hbm, gc_hbm, gr_ref, p_hbm,
    xb, cb, ab, xs, cv, gn, gc, pf, st, s1, s2, row_a, row_b, p_ref, x_sem, c_sem, a_sem, g_sem, p_sem,
):
    frames, width = xb.shape
    tiles = width // LANES
    rows = frames // SUB
    chunks = x_sem.shape[0]
    per_chunk = tiles // chunks
    per_group = p_ref.shape[2] // LANES
    block = 8

    def lanes_of(tile):
        return pl.ds(pl.multiple_of(tile * LANES, LANES), LANES)

    def chunk_lanes(chunk):
        wide = per_chunk * LANES
        return pl.ds(pl.multiple_of(chunk * wide, wide), wide)

    def x_copy(chunk):
        return pltpu.make_async_copy(
            x_hbm.at[:, chunk_lanes(chunk)], xb.at[:, chunk_lanes(chunk)], x_sem.at[chunk]
        )

    def c_copy(chunk):
        return pltpu.make_async_copy(
            ct_hbm.at[:, chunk_lanes(chunk)], cb.at[:, chunk_lanes(chunk)], c_sem.at[chunk]
        )

    def a_copy(chunk):
        return pltpu.make_async_copy(
            ab.at[:, chunk_lanes(chunk)], act_hbm.at[:, chunk_lanes(chunk)], a_sem.at[chunk]
        )

    def g_copy(chunk):
        at = pl.ds(chunk * per_chunk, per_chunk)
        return pltpu.make_async_copy(gc.at[at], gc_hbm.at[at], g_sem.at[chunk])

    for chunk in range(chunks):
        x_copy(chunk).start()
    for chunk in range(chunks):
        c_copy(chunk).start()
    place_params((p0, p1, p2, p3), at_ref[0], at_ref[1], p_ref)
    p_copy = pltpu.make_async_copy(p_ref, p_hbm, p_sem)
    p_copy.start()
    st[...] = jnp.zeros_like(st)

    def load_params(tile):
        group = tile // per_group
        inside = tile - group * per_group
        lanes = pl.ds(pl.multiple_of(inside * LANES, LANES), LANES)
        pf[...] = p_ref[group, :, lanes].astype(F32)

    zero = jnp.zeros((SUB, LANES), F32)
    s1[...] = jnp.zeros_like(s1)
    s2[...] = jnp.zeros_like(s2)

    def conv_tile(tile, _):
        load_params(tile)
        for edge in (0, SUB, PAD + frames, PAD + frames + SUB):
            xs[tile, pl.ds(edge, SUB), :] = zero
            gc[tile, pl.ds(edge, SUB), :] = zero
        xs[tile, pl.ds(PAD, frames), :] = xb[:, lanes_of(tile)].astype(F32)
        weights = [bcast_row(pf, j) for j in range(taps)]
        bias = bcast_row(pf, taps)
        for r0 in range(0, rows, block):
            acc = [bias] * block
            for phase in range(SUB):
                depth = len(range(phase, taps, SUB))
                for i in range(block + depth - 1):
                    value = xs[tile, pl.ds(SUB * (r0 + i) + phase + 1, SUB), :]
                    for q in range(depth):
                        if 0 <= i - q < block:
                            acc[i - q] = acc[i - q] + value * weights[phase + SUB * q]
            for b in range(block):
                at = pl.ds(SUB * (r0 + b), SUB)
                cv[tile, at, :] = acc[b]
                s1[at, :] += acc[b]
        return 0

    def conv_chunk(chunk, _):
        x_copy(chunk).wait()
        lax.fori_loop(chunk * per_chunk, (chunk + 1) * per_chunk, conv_tile, 0)
        return 0

    lax.fori_loop(0, chunks, conv_chunk, 0)

    row_a[...] = jnp.broadcast_to(
        jnp.sum(s1[...], axis=1, keepdims=True) * (1.0 / width), s1.shape
    )

    def var_tile(tile, _):
        for r in range(rows):
            at = pl.ds(SUB * r, SUB)
            off = cv[tile, at, :] - row_a[at, :]
            s2[at, :] += off * off
        return 0

    lax.fori_loop(0, tiles, var_tile, 0)
    row_b[...] = jnp.broadcast_to(
        lax.rsqrt(jnp.sum(s2[...], axis=1, keepdims=True) * (1.0 / width) + 1e-05), s2.shape
    )
    s1[...] = jnp.zeros_like(s1)
    s2[...] = jnp.zeros_like(s2)

    def act_tile(tile, _):
        load_params(tile)
        gain = bcast_row(pf, taps + 1)
        shift = bcast_row(pf, taps + 2)
        sum_gain, sum_shift = zero, zero
        for r0 in range(0, rows, 4):
            outs = []
            span = pl.ds(SUB * r0, SUB * 4)
            upstream = cb[span, lanes_of(tile)].astype(F32)
            for b in range(4):
                at = pl.ds(SUB * (r0 + b), SUB)
                normed = (cv[tile, at, :] - row_a[at, :]) * row_b[at, :]
                affine = gain * normed + shift
                squash = 0.5 * jnp.tanh(0.5 * affine) + 0.5
                act = affine * squash
                outs.append(act)
                ga = upstream[SUB * b : SUB * (b + 1)] * (squash * (1.0 + (affine - act)))
                sum_gain = sum_gain + ga * normed
                sum_shift = sum_shift + ga
                scaled = ga * gain
                cv[tile, at, :] = normed
                gn[tile, at, :] = scaled
                s1[at, :] += scaled
                s2[at, :] += scaled * normed
            ab[span, lanes_of(tile)] = jnp.concatenate(outs, 0).astype(ab.dtype)
        st[tile, pl.ds(taps + 1, 1), :] = jnp.sum(sum_gain, axis=0, keepdims=True)
        st[tile, pl.ds(taps + 2, 1), :] = jnp.sum(sum_shift, axis=0, keepdims=True)
        return 0

    def act_chunk(chunk, _):
        c_copy(chunk).wait()
        lax.fori_loop(chunk * per_chunk, (chunk + 1) * per_chunk, act_tile, 0)
        a_copy(chunk).start()
        return 0

    lax.fori_loop(0, chunks, act_chunk, 0)

    mean_gn = jnp.sum(s1[...], axis=1, keepdims=True) * (1.0 / width)
    mean_gnn = jnp.sum(s2[...], axis=1, keepdims=True) * (1.0 / width)
    s1[...] = jnp.broadcast_to(mean_gn, s1.shape)
    s2[...] = jnp.broadcast_to(mean_gnn, s2.shape)

    def grad_tile(tile, _):
        acc = [zero] * taps
        total = zero
        for r0 in range(0, rows, block):
            held = []
            for b in range(block):
                at = pl.ds(SUB * (r0 + b), SUB)
                grad = row_b[at, :] * (
                    gn[tile, at, :] - s1[at, :] - cv[tile, at, :] * s2[at, :]
                )
                gc[tile, pl.ds(PAD + SUB * (r0 + b), SUB), :] = grad
                total = total + grad
                held.append(grad)
            for phase in range(SUB):
                depth = len(range(phase, taps, SUB))
                for i in range(block + depth - 1):
                    value = xs[tile, pl.ds(SUB * (r0 + i) + phase + 1, SUB), :]
                    for q in range(depth):
                        if 0 <= i - q < block:
                            acc[phase + SUB * q] = acc[phase + SUB * q] + value * held[i - q]
        for j in range(taps):
            st[tile, pl.ds(j, 1), :] = jnp.sum(acc[j], axis=0, keepdims=True)
        st[tile, pl.ds(taps, 1), :] = jnp.sum(total, axis=0, keepdims=True)
        return 0

    def grad_chunk(chunk, _):
        lax.fori_loop(chunk * per_chunk, (chunk + 1) * per_chunk, grad_tile, 0)
        g_copy(chunk).start()
        return 0

    lax.fori_loop(0, chunks, grad_chunk, 0)

    def out_group(group, _):
        whole = jnp.concatenate(
            [st[group * per_group + u, :, :] for u in range(per_group)], axis=1
        )
        part = per_group * LANES // SIDE
        for a in range(SIDE):
            piece = whole[:, a * part : (a + 1) * part]
            spill = piece[MAIN : MAIN + SUB]
            width_left = LANES - part
            side = [spill[:, c : c + width_left] for c in range(0, part, width_left)]
            side.append(jnp.zeros((SUB, width_left), F32))
            both = jnp.concatenate([piece[:MAIN], jnp.concatenate(side, 0)], axis=1)
            at_yx = lax.rem(group, SIDE) * SIDE + a
            gr_ref[at_yx * SIDE + group // SIDE] = both
        return 0

    lax.fori_loop(0, tiles // per_group, out_group, 0)
    for chunk in range(chunks):
        a_copy(chunk).wait()
        g_copy(chunk).wait()
    p_copy.wait()


def input_grad(taps, chunks, gc_hbm, p_ref, *refs):
    gi_hbm, zero_ref, gc, gb, pf, g_sem, o_sem = refs[-7:]
    rows = gb.shape[0] // SUB
    per_chunk = CHUNK_TILES
    per_group = p_ref.shape[2] // LANES
    block = 8

    def g_copy(chunk):
        at = pl.ds(chunk * per_chunk, per_chunk)
        return pltpu.make_async_copy(gc_hbm.at[at], gc.at[at], g_sem.at[chunk])

    def o_copy(chunk):
        wide = per_chunk * LANES
        at = pl.ds(pl.multiple_of(chunk * wide, wide), wide)
        return pltpu.make_async_copy(gb.at[:, at], gi_hbm.at[:, at], o_sem.at[chunk])

    for chunk in range(*chunks):
        g_copy(chunk).start()
    zero_ref[...] = jnp.zeros_like(zero_ref)

    def tile_step(tile, _):
        group = tile // per_group
        inside = tile - group * per_group
        lanes = pl.ds(pl.multiple_of(inside * LANES, LANES), LANES)
        pf[...] = p_ref[group, :, lanes].astype(F32)
        weights = [bcast_row(pf, taps - 1 - j) for j in range(taps)]
        for r0 in range(0, rows, block):
            acc = [None] * block
            for phase in range(SUB):
                depth = len(range(phase, taps, SUB))
                for i in range(block + depth - 1):
                    value = gc[tile, pl.ds(SUB * (r0 + i) + phase + 1, SUB), :]
                    for q in range(depth):
                        b = i - q
                        if 0 <= b < block:
                            term = value * weights[phase + SUB * q]
                            acc[b] = term if acc[b] is None else acc[b] + term
            at = pl.ds(pl.multiple_of(tile * LANES, LANES), LANES)
            gb[pl.ds(SUB * r0, SUB * block), at] = jnp.concatenate(acc, 0).astype(gb.dtype)
        return 0

    def chunk_step(chunk, _):
        g_copy(chunk).wait()
        lax.fori_loop(chunk * per_chunk, (chunk + 1) * per_chunk, tile_step, 0)
        o_copy(chunk).start()
        return 0

    lax.fori_loop(*chunks, chunk_step, 0)
    for chunk in range(*chunks):
        o_copy(chunk).wait()


def sum_plane(at_ref, came_ref, zero_ref, *sum_refs):
    for step, sum_ref in enumerate(sum_refs):
        at = lax.rem(at_ref[0] + step, SIDE)
        total = zero_ref[...]
        for source in range(came_ref.shape[0]):
            total = total + came_ref[source, at]
        sum_ref[...] = total


def sum_column(own, first, second, third, zero_ref, sum_ref):
    sum_ref[...] = (own[...] + first[...]) + (second[...] + third[...]) + zero_ref[...]


def finish(scale, part, own, first, second, third, kernel_ref, bias_ref, gain_ref, shift_ref):
    total = ((own[...] + first[...]) + (second[...] + third[...])) * scale
    taps = kernel_ref.shape[0]
    kernel_ref[...] = total[:taps, :part]
    bias_ref[...] = total[taps : taps + 1, :part]
    for row, ref in ((0, gain_ref), (1, shift_ref)):
        ref[...] = jnp.concatenate(
            [total[SUB * c + row : SUB * c + row + 1, part:] for c in range(3)], axis=1
        )


ANY = pl.BlockSpec(memory_space=pl.ANY)
HELD = pl.BlockSpec(memory_space=pltpu.VMEM)


def run_first(x, cotangent, place, params, taps):
    frames, width = x.shape
    tiles = width // LANES
    chunks = 8
    rows = params[0].shape[1]
    groups = (SIDE * SIDE,) + params[0].shape[1:]
    padded = frames + 2 * PAD
    whole = (tiles, frames, LANES)
    return pl.pallas_call(
        functools.partial(forward_and_kernel_grad, taps),
        out_shape=(
            jax.ShapeDtypeStruct((frames, width), jnp.bfloat16),
            jax.ShapeDtypeStruct((tiles, padded, LANES), F32),
            jax.ShapeDtypeStruct((SIDE**3, MAIN, LANES), F32),
            jax.ShapeDtypeStruct(groups, params[0].dtype),
        ),
        in_specs=[pl.BlockSpec(memory_space=pltpu.SMEM), ANY, ANY] + [HELD] * SIDE,
        out_specs=(ANY, ANY, HELD, ANY),
        scratch_shapes=[
            pltpu.VMEM((frames, width), jnp.bfloat16),
            pltpu.VMEM((frames, width), jnp.bfloat16),
            pltpu.VMEM((frames, width), jnp.bfloat16),
            pltpu.VMEM((tiles, padded, LANES), F32),
            pltpu.VMEM(whole, F32),
            pltpu.VMEM(whole, F32),
            pltpu.VMEM((tiles, padded, LANES), F32),
            pltpu.VMEM((rows, LANES), F32),
            pltpu.VMEM((tiles, MAIN + SUB, LANES), F32),
            pltpu.VMEM((frames, LANES), F32),
            pltpu.VMEM((frames, LANES), F32),
            pltpu.VMEM((frames, LANES), F32),
            pltpu.VMEM((frames, LANES), F32),
            pltpu.VMEM(groups, params[0].dtype),
            pltpu.SemaphoreType.DMA((chunks,)),
            pltpu.SemaphoreType.DMA((chunks,)),
            pltpu.SemaphoreType.DMA((chunks,)),
            pltpu.SemaphoreType.DMA((chunks,)),
            pltpu.SemaphoreType.DMA,
        ],
        compiler_params=pltpu.CompilerParams(vmem_limit_bytes=52 << 20),
        cost_estimate=pl.CostEstimate(
            flops=4 * taps * frames * width, bytes_accessed=20 * frames * width, transcendentals=0
        ),
        name="forward_and_kernel_grad",
    )(place, x, cotangent, *params)


def run_second(grad_conv, params, taps, frames, width, chunks, begun=None):
    tiles = width // LANES
    share = (chunks[1] - chunks[0]) * CHUNK_TILES / tiles
    count = tiles // CHUNK_TILES
    return pl.pallas_call(
        functools.partial(input_grad, taps, chunks),
        out_shape=(
            jax.ShapeDtypeStruct((frames, width), jnp.bfloat16),
            jax.ShapeDtypeStruct((MAIN, LANES), F32),
        ),
        in_specs=[ANY, HELD] + ([] if begun is None else [ANY]),
        out_specs=(ANY, HELD),
        scratch_shapes=[
            pltpu.VMEM(grad_conv.shape, F32),
            pltpu.VMEM((frames, width), jnp.bfloat16),
            pltpu.VMEM((params.shape[1], LANES), F32),
            pltpu.SemaphoreType.DMA((count,)),
            pltpu.SemaphoreType.DMA((count,)),
        ],
        input_output_aliases={} if begun is None else {2: 0},
        compiler_params=pltpu.CompilerParams(vmem_limit_bytes=52 << 20),
        cost_estimate=pl.CostEstimate(
            flops=int(2 * taps * frames * width * share),
            bytes_accessed=int(6 * frames * width * share),
            transcendentals=0,
        ),
        name="input_grad",
    )(grad_conv, params, *([] if begun is None else [begun]))


def small(body, out_shape, name, *operands, scalars=0):
    scalar = pl.BlockSpec(memory_space=pltpu.SMEM)
    many = isinstance(out_shape, tuple)
    return pl.pallas_call(
        body,
        out_shape=out_shape,
        in_specs=[scalar] * scalars + [HELD] * (len(operands) - scalars),
        out_specs=(HELD,) * len(out_shape) if many else HELD,
        compiler_params=pltpu.CompilerParams(vmem_limit_bytes=8 << 20),
        name=name,
    )(*operands)


def over_rep(block, step):
    return lax.ppermute(block, "rep", [(i, i ^ step) for i in range(4)])


def per_device(conv_input, cotangent, kernel, conv_bias, ln_gain, ln_bias):
    taps = kernel.shape[0]
    clips, frames, width = conv_input.shape
    packed = jnp.concatenate([kernel, conv_bias[None], ln_gain[None], ln_bias[None]], 0)
    params = gather_channels(packed)
    me = lax.axis_index("shard")
    place = jnp.stack([me // (SIDE * SIDE), (me // SIDE) % SIDE])
    activated, grad_conv, pieces, groups = run_first(
        conv_input[0], cotangent[0], place, params, taps
    )
    part_of = functools.partial(run_second, grad_conv, groups, taps, frames, width)
    planes = [list(range(z * SIDE * SIDE, (z + 1) * SIDE * SIDE)) for z in range(SIDE)]
    came = lax.all_to_all(
        pieces.reshape(SIDE * SIDE, SIDE, MAIN, LANES), "shard", 0, 0, axis_index_groups=planes
    )
    begun, zeros = part_of((0, EARLY))
    piece = jax.ShapeDtypeStruct(zeros.shape, F32)
    sums = small(sum_plane, (piece,) * SIDE, "sum_plane", place, came, zeros, scalars=1)
    column = [lax.ppermute(sums[s], "shard", shifted(SIDE * SIDE, s)) for s in range(1, SIDE)]
    grad_input, zeros = part_of((EARLY, width // LANES // CHUNK_TILES), begun)
    own = small(sum_column, piece, "sum_column", sums[0], *column, zeros)
    others = [over_rep(own, step) for step in (1, 2, 3)]
    count = clips * frames * lax.axis_size("rep") * lax.axis_size("shard")
    part = packed.shape[1]
    row = jax.ShapeDtypeStruct((1, part), F32)
    grads = small(
        functools.partial(finish, 1.0 / math.sqrt(count), part),
        (jax.ShapeDtypeStruct((taps, part), F32), row, row, row),
        "finish", own, *others,
    )
    return (activated[None], grad_input[None], grads[0]) + tuple(g[0] for g in grads[1:])


def solution(mesh):
    data = P(("rep", "shard"), None, None)
    wide = P(None, "shard")
    narrow = P("shard")
    return jax.shard_map(
        per_device,
        mesh=mesh,
        in_specs=(data, data, wide, narrow, narrow, narrow),
        out_specs=(data, data, wide, narrow, narrow, narrow),
        check_vma=False,
    )
```

```python
import functools
import math

import jax
import jax.numpy as jnp
from jax import lax
from jax.experimental import pallas as pl
from jax.experimental.pallas import tpu as pltpu
from jax.sharding import PartitionSpec as P

SIDE = 4
LANES = 128
SUB = 8
PAD = 16
F32 = jnp.float32
CHUNK_TILES = 3
EARLY = 12
MAIN = 32


def shifted(axis_stride, step):
    pairs = []
    for source in range(SIDE**3):
        at = (source // axis_stride) % SIDE
        pairs.append((source, source + ((at + step) % SIDE - at) * axis_stride))
    return pairs


def plane_groups():
    plane = SIDE * SIDE
    return [list(range(z * plane, (z + 1) * plane)) for z in range(SIDE)]


def gather_channels(packed):
    stride = SIDE * SIDE
    column = jnp.concatenate(
        [packed] + [lax.ppermute(packed, "shard", shifted(stride, step)) for step in range(1, SIDE)]
    )
    same = jnp.broadcast_to(column[None], (stride,) + column.shape)
    return lax.all_to_all(same, "shard", 0, 0, axis_index_groups=plane_groups())


def place_params(came, at_z, p_ref):
    rows = p_ref.shape[1]
    for y in range(SIDE):
        for slot in range(SIDE):
            group = lax.rem(at_z - slot + SIDE, SIDE) * SIDE + y
            at = slice(slot * rows, (slot + 1) * rows)
            p_ref[group] = jnp.concatenate(
                [came[y * SIDE + x, at, :] for x in range(SIDE)], axis=1
            )


def bcast_row(ref, row):
    return jnp.broadcast_to(ref[pl.ds(row, 1), :], (SUB, LANES))


def forward_and_kernel_grad(
    taps, at_ref, x_hbm, ct_hbm, came_ref, act_hbm, gc_hbm, gr_ref, p_hbm,
    xb, cb, ab, xs, xe, xo, xt, fa, fb, fc, cv, gn, gc, pf, st, s1, s2, row_a, row_b, p_ref, x_sem, c_sem, a_sem, g_sem, p_sem,
):
    frames, width = xb.shape
    tiles = width // LANES
    rows = frames // SUB
    chunks = x_sem.shape[0]
    per_chunk = tiles // chunks
    per_group = p_ref.shape[2] // LANES
    block = 8

    def lanes_of(tile):
        return pl.ds(pl.multiple_of(tile * LANES, LANES), LANES)

    def chunk_lanes(chunk):
        wide = per_chunk * LANES
        return pl.ds(pl.multiple_of(chunk * wide, wide), wide)

    def x_copy(chunk):
        return pltpu.make_async_copy(
            x_hbm.at[:, chunk_lanes(chunk)], xb.at[:, chunk_lanes(chunk)], x_sem.at[chunk]
        )

    def c_copy(chunk):
        return pltpu.make_async_copy(
            ct_hbm.at[:, chunk_lanes(chunk)], cb.at[:, chunk_lanes(chunk)], c_sem.at[chunk]
        )

    def a_copy(chunk):
        return pltpu.make_async_copy(
            ab.at[:, chunk_lanes(chunk)], act_hbm.at[:, chunk_lanes(chunk)], a_sem.at[chunk]
        )

    def g_copy(chunk):
        at = pl.ds(chunk * per_chunk, per_chunk)
        return pltpu.make_async_copy(gc.at[at], gc_hbm.at[at], g_sem.at[chunk])

    for chunk in range(chunks):
        x_copy(chunk).start()
    for chunk in range(chunks):
        c_copy(chunk).start()
    place_params(came_ref, at_ref[0], p_ref)
    p_copy = pltpu.make_async_copy(p_ref, p_hbm, p_sem)
    p_copy.start()
    st[...] = jnp.zeros_like(st)

    def load_params(tile):
        group = tile // per_group
        inside = tile - group * per_group
        lanes = pl.ds(pl.multiple_of(inside * LANES, LANES), LANES)
        pf[...] = p_ref[group, :, lanes].astype(F32)

    zero = jnp.zeros((SUB, LANES), F32)
    s1[...] = jnp.zeros_like(s1)
    s2[...] = jnp.zeros_like(s2)

    for edge in (0, SUB, PAD + frames, PAD + frames + SUB, PAD + frames + 2 * SUB):
        xs[pl.ds(edge, SUB), :] = zero

    def conv_tile(tile, _):
        load_params(tile)
        for edge in (0, SUB, PAD + frames, PAD + frames + SUB):
            gc[tile, pl.ds(edge, SUB), :] = zero
        xs[pl.ds(PAD, frames), :] = xb[:, lanes_of(tile)].astype(F32)
        half = rows // 2
        xo[tile, pl.ds(SUB * (half + 2), SUB), :] = zero
        for r in range(half + 2):
            at = pl.ds(SUB * r, SUB)
            even = xs[pl.ds(2 * SUB * r + 1, SUB, stride=2), :]
            odd = xs[pl.ds(2 * SUB * r + 2, SUB, stride=2), :]
            xe[tile, at, :] = even
            xo[tile, at, :] = odd
            xt[tile, at, :] = even + odd
        bias = bcast_row(pf, taps)

        def run(source, weights, first, count, start, store):
            for r0 in range(0, count, block):
                size = min(block, count - r0)
                acc = [start] * size
                for phase in range(SUB):
                    depth = len(range(phase, len(weights), SUB))
                    for i in range(size + depth - 1):
                        value = source[tile, pl.ds(SUB * (r0 + i) + phase + first, SUB), :]
                        for q in range(depth):
                            if 0 <= i - q < size:
                                term = value * weights[phase + SUB * q]
                                before = acc[i - q]
                                acc[i - q] = term if before is None else before + term
                for b in range(size):
                    store(r0 + b, acc[b])

        w_even = [bcast_row(pf, 2 * e) for e in range(taps // 2 + 1)]
        w_odd = [bcast_row(pf, 2 * e + 1) for e in range(taps // 2)]

        def keep(ref):
            def store(r, value):
                ref[pl.ds(SUB * r, SUB), :] = value
            return store

        run(xo, w_odd, 0, half + 1, None, keep(fb))
        run(xe, w_even, 0, half, bias, keep(fa))
        w_both = [w_even[0]] + [w_even[e] + w_odd[e - 1] for e in range(1, len(w_even))]

        def last(r, value):
            here = pl.ds(SUB * r, SUB)
            own, before, after = fa[here, :], fb[here, :], fb[pl.ds(SUB * r + 1, SUB), :]
            cv[tile, pl.ds(2 * SUB * r, SUB, stride=2), :] = own + before
            cv[tile, pl.ds(2 * SUB * r + 1, SUB, stride=2), :] = (value - own) - after + (bias + bias)

        run(xt, w_both, 0, half, None, last)
        for r in range(rows):
            at = pl.ds(SUB * r, SUB)
            s1[at, :] += cv[tile, at, :]
        return 0

    def conv_chunk(chunk, _):
        x_copy(chunk).wait()
        lax.fori_loop(chunk * per_chunk, (chunk + 1) * per_chunk, conv_tile, 0)
        return 0

    lax.fori_loop(0, chunks, conv_chunk, 0)

    row_a[...] = jnp.broadcast_to(
        jnp.sum(s1[...], axis=1, keepdims=True) * (1.0 / width), s1.shape
    )

    def var_tile(tile, _):
        for r in range(rows):
            at = pl.ds(SUB * r, SUB)
            off = cv[tile, at, :] - row_a[at, :]
            s2[at, :] += off * off
        return 0

    lax.fori_loop(0, tiles, var_tile, 0)
    row_b[...] = jnp.broadcast_to(
        lax.rsqrt(jnp.sum(s2[...], axis=1, keepdims=True) * (1.0 / width) + 1e-05), s2.shape
    )
    s1[...] = jnp.zeros_like(s1)
    s2[...] = jnp.zeros_like(s2)

    def act_tile(tile, _):
        load_params(tile)
        gain = bcast_row(pf, taps + 1)
        shift = bcast_row(pf, taps + 2)
        sum_gain, sum_shift = zero, zero
        for r0 in range(0, rows, 4):
            outs = []
            span = pl.ds(SUB * r0, SUB * 4)
            upstream = cb[span, lanes_of(tile)].astype(F32)
            for b in range(4):
                at = pl.ds(SUB * (r0 + b), SUB)
                normed = (cv[tile, at, :] - row_a[at, :]) * row_b[at, :]
                affine = gain * normed + shift
                squash = 0.5 * jnp.tanh(0.5 * affine) + 0.5
                act = affine * squash
                outs.append(act)
                ga = upstream[SUB * b : SUB * (b + 1)] * (squash * (1.0 + (affine - act)))
                sum_gain = sum_gain + ga * normed
                sum_shift = sum_shift + ga
                scaled = ga * gain
                cv[tile, at, :] = normed
                gn[tile, at, :] = scaled
                s1[at, :] += scaled
                s2[at, :] += scaled * normed
            ab[span, lanes_of(tile)] = jnp.concatenate(outs, 0).astype(ab.dtype)
        st[tile, pl.ds(taps + 1, 1), :] = jnp.sum(sum_gain, axis=0, keepdims=True)
        st[tile, pl.ds(taps + 2, 1), :] = jnp.sum(sum_shift, axis=0, keepdims=True)
        return 0

    def act_chunk(chunk, _):
        c_copy(chunk).wait()
        lax.fori_loop(chunk * per_chunk, (chunk + 1) * per_chunk, act_tile, 0)
        a_copy(chunk).start()
        return 0

    lax.fori_loop(0, chunks, act_chunk, 0)

    mean_gn = jnp.sum(s1[...], axis=1, keepdims=True) * (1.0 / width)
    mean_gnn = jnp.sum(s2[...], axis=1, keepdims=True) * (1.0 / width)
    s1[...] = jnp.broadcast_to(mean_gn, s1.shape)
    s2[...] = jnp.broadcast_to(mean_gnn, s2.shape)

    def grad_tile(tile, _):
        total = zero
        for r0 in range(0, rows, block):
            for b in range(block):
                at = pl.ds(SUB * (r0 + b), SUB)
                grad = row_b[at, :] * (
                    gn[tile, at, :] - s1[at, :] - cv[tile, at, :] * s2[at, :]
                )
                gc[tile, pl.ds(PAD + SUB * (r0 + b), SUB), :] = grad
                total = total + grad
        half = rows // 2
        for r in range(half):
            here = pl.ds(SUB * r, SUB)
            g_even = gc[tile, pl.ds(PAD + 2 * SUB * r, SUB, stride=2), :]
            g_odd = gc[tile, pl.ds(PAD + 2 * SUB * r + 1, SUB, stride=2), :]
            fa[here, :] = g_even - g_odd
            fc[here, :] = g_odd
        for r in range(half + 1):
            g_even = gc[tile, pl.ds(PAD + 2 * SUB * r, SUB, stride=2), :]
            g_before = gc[tile, pl.ds(PAD + 2 * SUB * r - 1, SUB, stride=2), :]
            fb[pl.ds(SUB * r, SUB), :] = g_even - g_before

        def corr(source, grads, count, size):
            acc = [zero] * size
            for r0 in range(0, count, block):
                many = min(block, count - r0)
                held = [grads[pl.ds(SUB * (r0 + b), SUB), :] for b in range(many)]
                for phase in range(SUB):
                    depth = len(range(phase, size, SUB))
                    for i in range(many + depth - 1):
                        value = source[tile, pl.ds(SUB * (r0 + i) + phase, SUB), :]
                        for q in range(depth):
                            if 0 <= i - q < many:
                                acc[phase + SUB * q] = acc[phase + SUB * q] + value * held[i - q]
            return acc

        d_even = corr(xe, fa, half, taps // 2 + 1)
        d_both = corr(xt, fc, half, taps // 2 + 1)
        for e in range(taps // 2 + 1):
            st[tile, pl.ds(2 * e, 1), :] = jnp.sum(d_even[e] + d_both[e], axis=0, keepdims=True)
        d_odd = corr(xo, fb, half + 1, taps // 2)
        for e in range(taps // 2):
            both = d_odd[e] + d_both[e + 1]
            st[tile, pl.ds(2 * e + 1, 1), :] = jnp.sum(both, axis=0, keepdims=True)
        st[tile, pl.ds(taps, 1), :] = jnp.sum(total, axis=0, keepdims=True)
        return 0

    def grad_chunk(chunk, _):
        lax.fori_loop(chunk * per_chunk, (chunk + 1) * per_chunk, grad_tile, 0)
        g_copy(chunk).start()
        return 0

    lax.fori_loop(0, chunks, grad_chunk, 0)

    def out_group(group, _):
        whole = jnp.concatenate(
            [st[group * per_group + u, :, :] for u in range(per_group)], axis=1
        )
        part = per_group * LANES // SIDE
        for a in range(SIDE):
            piece = whole[:, a * part : (a + 1) * part]
            spill = piece[MAIN : MAIN + SUB]
            width_left = LANES - part
            side = [spill[:, c : c + width_left] for c in range(0, part, width_left)]
            side.append(jnp.zeros((SUB, width_left), F32))
            both = jnp.concatenate([piece[:MAIN], jnp.concatenate(side, 0)], axis=1)
            at_yx = lax.rem(group, SIDE) * SIDE + a
            gr_ref[at_yx * SIDE + group // SIDE] = both
        return 0

    lax.fori_loop(0, tiles // per_group, out_group, 0)
    for chunk in range(chunks):
        a_copy(chunk).wait()
        g_copy(chunk).wait()
    p_copy.wait()


def input_grad(taps, chunks, gc_hbm, p_ref, *refs):
    gi_hbm, zero_ref, gc, gb, pf, g_sem, o_sem = refs[-7:]
    rows = gb.shape[0] // SUB
    per_chunk = CHUNK_TILES
    per_group = p_ref.shape[2] // LANES
    block = 8

    def g_copy(chunk):
        at = pl.ds(chunk * per_chunk, per_chunk)
        return pltpu.make_async_copy(gc_hbm.at[at], gc.at[at], g_sem.at[chunk])

    def o_copy(chunk):
        wide = per_chunk * LANES
        at = pl.ds(pl.multiple_of(chunk * wide, wide), wide)
        return pltpu.make_async_copy(gb.at[:, at], gi_hbm.at[:, at], o_sem.at[chunk])

    for chunk in range(*chunks):
        g_copy(chunk).start()
    zero_ref[...] = jnp.zeros_like(zero_ref)

    def tile_step(tile, _):
        group = tile // per_group
        inside = tile - group * per_group
        lanes = pl.ds(pl.multiple_of(inside * LANES, LANES), LANES)
        pf[...] = p_ref[group, :, lanes].astype(F32)
        weights = [bcast_row(pf, taps - 1 - j) for j in range(taps)]
        for r0 in range(0, rows, block):
            acc = [None] * block
            for phase in range(SUB):
                depth = len(range(phase, taps, SUB))
                for i in range(block + depth - 1):
                    value = gc[tile, pl.ds(SUB * (r0 + i) + phase + 1, SUB), :]
                    for q in range(depth):
                        b = i - q
                        if 0 <= b < block:
                            term = value * weights[phase + SUB * q]
                            acc[b] = term if acc[b] is None else acc[b] + term
            at = pl.ds(pl.multiple_of(tile * LANES, LANES), LANES)
            gb[pl.ds(SUB * r0, SUB * block), at] = jnp.concatenate(acc, 0).astype(gb.dtype)
        return 0

    def chunk_step(chunk, _):
        g_copy(chunk).wait()
        lax.fori_loop(chunk * per_chunk, (chunk + 1) * per_chunk, tile_step, 0)
        o_copy(chunk).start()
        return 0

    lax.fori_loop(*chunks, chunk_step, 0)
    for chunk in range(*chunks):
        o_copy(chunk).wait()


def sum_plane(at_ref, came_ref, zero_ref, *sum_refs):
    for step, sum_ref in enumerate(sum_refs):
        at = lax.rem(at_ref[0] + step, SIDE)
        total = zero_ref[...]
        for source in range(came_ref.shape[0]):
            total = total + came_ref[source, at]
        sum_ref[...] = total


def sum_column(own, first, second, third, zero_ref, sum_ref):
    sum_ref[...] = (own[...] + first[...]) + (second[...] + third[...]) + zero_ref[...]


def finish(scale, part, own, first, second, third, kernel_ref, bias_ref, gain_ref, shift_ref):
    total = ((own[...] + first[...]) + (second[...] + third[...])) * scale
    taps = kernel_ref.shape[0]
    kernel_ref[...] = total[:taps, :part]
    bias_ref[...] = total[taps : taps + 1, :part]
    for row, ref in ((0, gain_ref), (1, shift_ref)):
        ref[...] = jnp.concatenate(
            [total[SUB * c + row : SUB * c + row + 1, part:] for c in range(3)], axis=1
        )


ANY = pl.BlockSpec(memory_space=pl.ANY)
HELD = pl.BlockSpec(memory_space=pltpu.VMEM)


def run_first(x, cotangent, place, params, taps):
    frames, width = x.shape
    tiles = width // LANES
    chunks = 8
    rows = params.shape[1] // SIDE
    groups = (SIDE * SIDE, rows, SIDE * params.shape[2])
    padded = frames + 2 * PAD
    whole = (tiles, frames, LANES)
    return pl.pallas_call(
        functools.partial(forward_and_kernel_grad, taps),
        out_shape=(
            jax.ShapeDtypeStruct((frames, width), jnp.bfloat16),
            jax.ShapeDtypeStruct((tiles, padded, LANES), F32),
            jax.ShapeDtypeStruct((SIDE**3, MAIN, LANES), F32),
            jax.ShapeDtypeStruct(groups, params.dtype),
        ),
        in_specs=[pl.BlockSpec(memory_space=pltpu.SMEM), ANY, ANY, HELD],
        out_specs=(ANY, ANY, HELD, ANY),
        scratch_shapes=[
            pltpu.VMEM((frames, width), jnp.bfloat16),
            pltpu.VMEM((frames, width), jnp.bfloat16),
            pltpu.VMEM((frames, width), jnp.bfloat16),
            pltpu.VMEM((padded + SUB, LANES), F32),
            pltpu.VMEM((tiles, frames // 2 + 3 * SUB, LANES), F32),
            pltpu.VMEM((tiles, frames // 2 + 3 * SUB, LANES), F32),
            pltpu.VMEM((tiles, frames // 2 + 3 * SUB, LANES), F32),
            pltpu.VMEM((frames // 2, LANES), F32),
            pltpu.VMEM((frames // 2 + SUB, LANES), F32),
            pltpu.VMEM((frames // 2, LANES), F32),
            pltpu.VMEM(whole, F32),
            pltpu.VMEM(whole, F32),
            pltpu.VMEM((tiles, padded, LANES), F32),
            pltpu.VMEM((rows, LANES), F32),
            pltpu.VMEM((tiles, MAIN + SUB, LANES), F32),
            pltpu.VMEM((frames, LANES), F32),
            pltpu.VMEM((frames, LANES), F32),
            pltpu.VMEM((frames, LANES), F32),
            pltpu.VMEM((frames, LANES), F32),
            pltpu.VMEM(groups, params.dtype),
            pltpu.SemaphoreType.DMA((chunks,)),
            pltpu.SemaphoreType.DMA((chunks,)),
            pltpu.SemaphoreType.DMA((chunks,)),
            pltpu.SemaphoreType.DMA((chunks,)),
            pltpu.SemaphoreType.DMA,
        ],
        compiler_params=pltpu.CompilerParams(vmem_limit_bytes=52 << 20),
        cost_estimate=pl.CostEstimate(
            flops=4 * taps * frames * width, bytes_accessed=20 * frames * width, transcendentals=0
        ),
        name="forward_and_kernel_grad",
    )(place, x, cotangent, params)


def run_second(grad_conv, params, taps, frames, width, chunks, begun=None):
    tiles = width // LANES
    share = (chunks[1] - chunks[0]) * CHUNK_TILES / tiles
    count = tiles // CHUNK_TILES
    return pl.pallas_call(
        functools.partial(input_grad, taps, chunks),
        out_shape=(
            jax.ShapeDtypeStruct((frames, width), jnp.bfloat16),
            jax.ShapeDtypeStruct((MAIN, LANES), F32),
        ),
        in_specs=[ANY, HELD] + ([] if begun is None else [ANY]),
        out_specs=(ANY, HELD),
        scratch_shapes=[
            pltpu.VMEM(grad_conv.shape, F32),
            pltpu.VMEM((frames, width), jnp.bfloat16),
            pltpu.VMEM((params.shape[1], LANES), F32),
            pltpu.SemaphoreType.DMA((count,)),
            pltpu.SemaphoreType.DMA((count,)),
        ],
        input_output_aliases={} if begun is None else {2: 0},
        compiler_params=pltpu.CompilerParams(vmem_limit_bytes=52 << 20),
        cost_estimate=pl.CostEstimate(
            flops=int(2 * taps * frames * width * share),
            bytes_accessed=int(6 * frames * width * share),
            transcendentals=0,
        ),
        name="input_grad",
    )(grad_conv, params, *([] if begun is None else [begun]))


def small(body, out_shape, name, *operands, scalars=0):
    scalar = pl.BlockSpec(memory_space=pltpu.SMEM)
    many = isinstance(out_shape, tuple)
    return pl.pallas_call(
        body,
        out_shape=out_shape,
        in_specs=[scalar] * scalars + [HELD] * (len(operands) - scalars),
        out_specs=(HELD,) * len(out_shape) if many else HELD,
        compiler_params=pltpu.CompilerParams(vmem_limit_bytes=8 << 20),
        name=name,
    )(*operands)


def over_rep(block, step):
    return lax.ppermute(block, "rep", [(i, i ^ step) for i in range(4)])


def per_device(conv_input, cotangent, kernel, conv_bias, ln_gain, ln_bias):
    taps = kernel.shape[0]
    clips, frames, width = conv_input.shape
    packed = jnp.concatenate([kernel, conv_bias[None], ln_gain[None], ln_bias[None]], 0)
    params = gather_channels(packed)
    me = lax.axis_index("shard")
    place = (me // (SIDE * SIDE))[None]
    activated, grad_conv, pieces, groups = run_first(
        conv_input[0], cotangent[0], place, params, taps
    )
    part_of = functools.partial(run_second, grad_conv, groups, taps, frames, width)
    came = lax.all_to_all(
        pieces.reshape(SIDE * SIDE, SIDE, MAIN, LANES), "shard", 0, 0, axis_index_groups=plane_groups()
    )
    begun, zeros = part_of((0, EARLY))
    piece = jax.ShapeDtypeStruct(zeros.shape, F32)
    sums = small(sum_plane, (piece,) * SIDE, "sum_plane", place, came, zeros, scalars=1)
    column = [lax.ppermute(sums[s], "shard", shifted(SIDE * SIDE, s)) for s in range(1, SIDE)]
    grad_input, zeros = part_of((EARLY, width // LANES // CHUNK_TILES), begun)
    own = small(sum_column, piece, "sum_column", sums[0], *column, zeros)
    others = [over_rep(own, step) for step in (1, 2, 3)]
    count = clips * frames * lax.axis_size("rep") * lax.axis_size("shard")
    part = packed.shape[1]
    row = jax.ShapeDtypeStruct((1, part), F32)
    grads = small(
        functools.partial(finish, 1.0 / math.sqrt(count), part),
        (jax.ShapeDtypeStruct((taps, part), F32), row, row, row),
        "finish", own, *others,
    )
    return (activated[None], grad_input[None], grads[0]) + tuple(g[0] for g in grads[1:])


def solution(mesh):
    data = P(("rep", "shard"), None, None)
    wide = P(None, "shard")
    narrow = P("shard")
    return jax.shard_map(
        per_device,
        mesh=mesh,
        in_specs=(data, data, wide, narrow, narrow, narrow),
        out_specs=(data, data, wide, narrow, narrow, narrow),
        check_vma=False,
    )
```

```python
import functools
import math

import jax
import jax.numpy as jnp
from jax import lax
from jax.experimental import pallas as pl
from jax.experimental.pallas import tpu as pltpu
from jax.sharding import PartitionSpec as P

SIDE = 4
LANES = 128
SUB = 8
PAD = 16
F32 = jnp.float32
CHUNK_TILES = 3
EARLY = 10
MAIN = 32


def shifted(axis_stride, step):
    pairs = []
    for source in range(SIDE**3):
        at = (source // axis_stride) % SIDE
        pairs.append((source, source + ((at + step) % SIDE - at) * axis_stride))
    return pairs


def plane_groups():
    plane = SIDE * SIDE
    return [list(range(z * plane, (z + 1) * plane)) for z in range(SIDE)]


def spread(*refs):
    out_ref = refs[-1]
    rows = refs[0].shape[0]
    for to in range(out_ref.shape[0]):
        for slot, ref in enumerate(refs[:-1]):
            out_ref[to, slot * rows : (slot + 1) * rows, :] = ref[...]


def gather_channels(packed):
    stride = SIDE * SIDE
    column = [packed] + [
        lax.ppermute(packed, "shard", shifted(stride, step)) for step in range(1, SIDE)
    ]
    shape = jax.ShapeDtypeStruct((stride, SIDE * packed.shape[0], packed.shape[1]), packed.dtype)
    same = small(spread, shape, "spread", *column)
    return lax.all_to_all(same, "shard", 0, 0, axis_index_groups=plane_groups())


def place_params(came, at_z, p_ref):
    rows = p_ref.shape[1]
    for y in range(SIDE):
        for slot in range(SIDE):
            group = lax.rem(at_z - slot + SIDE, SIDE) * SIDE + y
            at = slice(slot * rows, (slot + 1) * rows)
            p_ref[group] = jnp.concatenate(
                [came[y * SIDE + x, at, :] for x in range(SIDE)], axis=1
            )


def bcast_row(ref, row):
    return jnp.broadcast_to(ref[pl.ds(row, 1), :], (SUB, LANES))


def forward_and_kernel_grad(
    taps, at_ref, x_hbm, ct_hbm, came_ref, act_hbm, gc_hbm, gr_ref, p_hbm,
    xb, cb, ab, xs, xe, xo, xt, fa, fb, fc, cv, gn, gc, pf, st, s1, s2, row_a, row_b, p_ref, x_sem, c_sem, a_sem, g_sem, p_sem,
):
    frames, width = xb.shape
    tiles = width // LANES
    rows = frames // SUB
    chunks = x_sem.shape[0]
    per_chunk = tiles // chunks
    per_group = p_ref.shape[2] // LANES
    block = 8

    def lanes_of(tile):
        return pl.ds(pl.multiple_of(tile * LANES, LANES), LANES)

    def chunk_lanes(chunk):
        wide = per_chunk * LANES
        return pl.ds(pl.multiple_of(chunk * wide, wide), wide)

    def x_copy(chunk):
        return pltpu.make_async_copy(
            x_hbm.at[:, chunk_lanes(chunk)], xb.at[:, chunk_lanes(chunk)], x_sem.at[chunk]
        )

    def c_copy(chunk):
        return pltpu.make_async_copy(
            ct_hbm.at[:, chunk_lanes(chunk)], cb.at[:, chunk_lanes(chunk)], c_sem.at[chunk]
        )

    def a_copy(chunk):
        return pltpu.make_async_copy(
            ab.at[:, chunk_lanes(chunk)], act_hbm.at[:, chunk_lanes(chunk)], a_sem.at[chunk]
        )

    def g_copy(chunk):
        at = pl.ds(chunk * per_chunk, per_chunk)
        return pltpu.make_async_copy(gc.at[at], gc_hbm.at[at], g_sem.at[chunk])

    for chunk in range(chunks):
        x_copy(chunk).start()
    for chunk in range(chunks):
        c_copy(chunk).start()
    place_params(came_ref, at_ref[0], p_ref)
    p_copy = pltpu.make_async_copy(p_ref, p_hbm, p_sem)
    p_copy.start()
    st[...] = jnp.zeros_like(st)

    def load_params(tile):
        group = tile // per_group
        inside = tile - group * per_group
        lanes = pl.ds(pl.multiple_of(inside * LANES, LANES), LANES)
        pf[...] = p_ref[group, :, lanes].astype(F32)

    zero = jnp.zeros((SUB, LANES), F32)
    s1[...] = jnp.zeros_like(s1)
    s2[...] = jnp.zeros_like(s2)

    for edge in (0, SUB, PAD + frames, PAD + frames + SUB, PAD + frames + 2 * SUB):
        xs[pl.ds(edge, SUB), :] = zero

    def conv_tile(tile, _):
        load_params(tile)
        for edge in (0, SUB, PAD + frames, PAD + frames + SUB):
            gc[tile, pl.ds(edge, SUB), :] = zero
        xs[pl.ds(PAD, frames), :] = xb[:, lanes_of(tile)].astype(F32)
        half = rows // 2
        xo[tile, pl.ds(SUB * (half + 2), SUB), :] = zero
        for r in range(half + 2):
            at = pl.ds(SUB * r, SUB)
            even = xs[pl.ds(2 * SUB * r + 1, SUB, stride=2), :]
            odd = xs[pl.ds(2 * SUB * r + 2, SUB, stride=2), :]
            xe[tile, at, :] = even
            xo[tile, at, :] = odd
            xt[tile, at, :] = even + odd
        bias = bcast_row(pf, taps)

        def run(source, weights, first, count, start, store):
            for r0 in range(0, count, block):
                size = min(block, count - r0)
                acc = [start] * size
                for phase in range(SUB):
                    depth = len(range(phase, len(weights), SUB))
                    for i in range(size + depth - 1):
                        value = source[tile, pl.ds(SUB * (r0 + i) + phase + first, SUB), :]
                        for q in range(depth):
                            if 0 <= i - q < size:
                                term = value * weights[phase + SUB * q]
                                before = acc[i - q]
                                acc[i - q] = term if before is None else before + term
                for b in range(size):
                    store(r0 + b, acc[b])

        w_even = [bcast_row(pf, 2 * e) for e in range(taps // 2 + 1)]
        w_odd = [bcast_row(pf, 2 * e + 1) for e in range(taps // 2)]

        def keep(ref):
            def store(r, value):
                ref[pl.ds(SUB * r, SUB), :] = value
            return store

        run(xo, w_odd, 0, half + 1, None, keep(fb))
        run(xe, w_even, 0, half, bias, keep(fa))
        w_both = [w_even[0]] + [w_even[e] + w_odd[e - 1] for e in range(1, len(w_even))]

        def last(r, value):
            here = pl.ds(SUB * r, SUB)
            own, before, after = fa[here, :], fb[here, :], fb[pl.ds(SUB * r + 1, SUB), :]
            cv[tile, pl.ds(2 * SUB * r, SUB, stride=2), :] = own + before
            cv[tile, pl.ds(2 * SUB * r + 1, SUB, stride=2), :] = (value - own) - after + (bias + bias)

        run(xt, w_both, 0, half, None, last)
        for r in range(rows):
            at = pl.ds(SUB * r, SUB)
            s1[at, :] += cv[tile, at, :]
        return 0

    def conv_chunk(chunk, _):
        x_copy(chunk).wait()
        lax.fori_loop(chunk * per_chunk, (chunk + 1) * per_chunk, conv_tile, 0)
        return 0

    lax.fori_loop(0, chunks, conv_chunk, 0)

    row_a[...] = jnp.broadcast_to(
        jnp.sum(s1[...], axis=1, keepdims=True) * (1.0 / width), s1.shape
    )

    def var_tile(tile, _):
        for r in range(rows):
            at = pl.ds(SUB * r, SUB)
            off = cv[tile, at, :] - row_a[at, :]
            s2[at, :] += off * off
        return 0

    lax.fori_loop(0, tiles, var_tile, 0)
    row_b[...] = jnp.broadcast_to(
        lax.rsqrt(jnp.sum(s2[...], axis=1, keepdims=True) * (1.0 / width) + 1e-05), s2.shape
    )
    s1[...] = jnp.zeros_like(s1)
    s2[...] = jnp.zeros_like(s2)

    def act_tile(tile, _):
        load_params(tile)
        gain = bcast_row(pf, taps + 1)
        shift = bcast_row(pf, taps + 2)
        sum_gain, sum_shift = zero, zero
        for r0 in range(0, rows, 4):
            outs = []
            span = pl.ds(SUB * r0, SUB * 4)
            upstream = cb[span, lanes_of(tile)].astype(F32)
            for b in range(4):
                at = pl.ds(SUB * (r0 + b), SUB)
                normed = (cv[tile, at, :] - row_a[at, :]) * row_b[at, :]
                affine = gain * normed + shift
                squash = 0.5 * jnp.tanh(0.5 * affine) + 0.5
                act = affine * squash
                outs.append(act)
                ga = upstream[SUB * b : SUB * (b + 1)] * (squash * (1.0 + (affine - act)))
                sum_gain = sum_gain + ga * normed
                sum_shift = sum_shift + ga
                scaled = ga * gain
                cv[tile, at, :] = normed
                gn[tile, at, :] = scaled
                s1[at, :] += scaled
                s2[at, :] += scaled * normed
            ab[span, lanes_of(tile)] = jnp.concatenate(outs, 0).astype(ab.dtype)
        st[tile, pl.ds(taps + 1, 1), :] = jnp.sum(sum_gain, axis=0, keepdims=True)
        st[tile, pl.ds(taps + 2, 1), :] = jnp.sum(sum_shift, axis=0, keepdims=True)
        return 0

    def act_chunk(chunk, _):
        c_copy(chunk).wait()
        lax.fori_loop(chunk * per_chunk, (chunk + 1) * per_chunk, act_tile, 0)
        a_copy(chunk).start()
        return 0

    lax.fori_loop(0, chunks, act_chunk, 0)

    mean_gn = jnp.sum(s1[...], axis=1, keepdims=True) * (1.0 / width)
    mean_gnn = jnp.sum(s2[...], axis=1, keepdims=True) * (1.0 / width)
    s1[...] = jnp.broadcast_to(mean_gn, s1.shape)
    s2[...] = jnp.broadcast_to(mean_gnn, s2.shape)

    def grad_tile(tile, _):
        total = zero
        for r0 in range(0, rows, block):
            for b in range(block):
                at = pl.ds(SUB * (r0 + b), SUB)
                grad = row_b[at, :] * (
                    gn[tile, at, :] - s1[at, :] - cv[tile, at, :] * s2[at, :]
                )
                gc[tile, pl.ds(PAD + SUB * (r0 + b), SUB), :] = grad
                total = total + grad
        half = rows // 2
        for r in range(half):
            here = pl.ds(SUB * r, SUB)
            g_even = gc[tile, pl.ds(PAD + 2 * SUB * r, SUB, stride=2), :]
            g_odd = gc[tile, pl.ds(PAD + 2 * SUB * r + 1, SUB, stride=2), :]
            fa[here, :] = g_even - g_odd
            fc[here, :] = g_odd
        for r in range(half + 1):
            g_even = gc[tile, pl.ds(PAD + 2 * SUB * r, SUB, stride=2), :]
            g_before = gc[tile, pl.ds(PAD + 2 * SUB * r - 1, SUB, stride=2), :]
            fb[pl.ds(SUB * r, SUB), :] = g_even - g_before

        def corr(source, grads, count, size):
            acc = [zero] * size
            for r0 in range(0, count, block):
                many = min(block, count - r0)
                held = [grads[pl.ds(SUB * (r0 + b), SUB), :] for b in range(many)]
                for phase in range(SUB):
                    depth = len(range(phase, size, SUB))
                    for i in range(many + depth - 1):
                        value = source[tile, pl.ds(SUB * (r0 + i) + phase, SUB), :]
                        for q in range(depth):
                            if 0 <= i - q < many:
                                acc[phase + SUB * q] = acc[phase + SUB * q] + value * held[i - q]
            return acc

        d_even = corr(xe, fa, half, taps // 2 + 1)
        d_both = corr(xt, fc, half, taps // 2 + 1)
        for e in range(taps // 2 + 1):
            st[tile, pl.ds(2 * e, 1), :] = jnp.sum(d_even[e] + d_both[e], axis=0, keepdims=True)
        d_odd = corr(xo, fb, half + 1, taps // 2)
        for e in range(taps // 2):
            both = d_odd[e] + d_both[e + 1]
            st[tile, pl.ds(2 * e + 1, 1), :] = jnp.sum(both, axis=0, keepdims=True)
        st[tile, pl.ds(taps, 1), :] = jnp.sum(total, axis=0, keepdims=True)
        return 0

    def grad_chunk(chunk, _):
        lax.fori_loop(chunk * per_chunk, (chunk + 1) * per_chunk, grad_tile, 0)
        g_copy(chunk).start()
        return 0

    lax.fori_loop(0, chunks, grad_chunk, 0)

    def out_group(group, _):
        whole = jnp.concatenate(
            [st[group * per_group + u, :, :] for u in range(per_group)], axis=1
        )
        part = per_group * LANES // SIDE
        for a in range(SIDE):
            piece = whole[:, a * part : (a + 1) * part]
            spill = piece[MAIN : MAIN + SUB]
            width_left = LANES - part
            side = [spill[:, c : c + width_left] for c in range(0, part, width_left)]
            side.append(jnp.zeros((SUB, width_left), F32))
            both = jnp.concatenate([piece[:MAIN], jnp.concatenate(side, 0)], axis=1)
            at_yx = lax.rem(group, SIDE) * SIDE + a
            gr_ref[at_yx * SIDE + group // SIDE] = both
        return 0

    lax.fori_loop(0, tiles // per_group, out_group, 0)
    for chunk in range(chunks):
        a_copy(chunk).wait()
        g_copy(chunk).wait()
    p_copy.wait()


def input_grad(taps, chunks, gc_hbm, p_ref, *refs):
    gi_hbm, zero_ref, gc, gb, pf, g_sem, o_sem = refs[-7:]
    rows = gb.shape[0] // SUB
    per_chunk = CHUNK_TILES
    per_group = p_ref.shape[2] // LANES
    block = 8

    def g_copy(chunk):
        at = pl.ds(chunk * per_chunk, per_chunk)
        return pltpu.make_async_copy(gc_hbm.at[at], gc.at[at], g_sem.at[chunk])

    def o_copy(chunk):
        wide = per_chunk * LANES
        at = pl.ds(pl.multiple_of(chunk * wide, wide), wide)
        return pltpu.make_async_copy(gb.at[:, at], gi_hbm.at[:, at], o_sem.at[chunk])

    for chunk in range(*chunks):
        g_copy(chunk).start()
    zero_ref[...] = jnp.zeros_like(zero_ref)

    def tile_step(tile, _):
        group = tile // per_group
        inside = tile - group * per_group
        lanes = pl.ds(pl.multiple_of(inside * LANES, LANES), LANES)
        pf[...] = p_ref[group, :, lanes].astype(F32)
        weights = [bcast_row(pf, taps - 1 - j) for j in range(taps)]
        for r0 in range(0, rows, block):
            acc = [None] * block
            for phase in range(SUB):
                depth = len(range(phase, taps, SUB))
                for i in range(block + depth - 1):
                    value = gc[tile, pl.ds(SUB * (r0 + i) + phase + 1, SUB), :]
                    for q in range(depth):
                        b = i - q
                        if 0 <= b < block:
                            term = value * weights[phase + SUB * q]
                            acc[b] = term if acc[b] is None else acc[b] + term
            at = pl.ds(pl.multiple_of(tile * LANES, LANES), LANES)
            gb[pl.ds(SUB * r0, SUB * block), at] = jnp.concatenate(acc, 0).astype(gb.dtype)
        return 0

    def chunk_step(chunk, _):
        g_copy(chunk).wait()
        lax.fori_loop(chunk * per_chunk, (chunk + 1) * per_chunk, tile_step, 0)
        o_copy(chunk).start()
        return 0

    lax.fori_loop(*chunks, chunk_step, 0)
    for chunk in range(*chunks):
        o_copy(chunk).wait()


def sum_plane(came_ref, zero_ref, sum_ref):
    for z in range(SIDE):
        total = zero_ref[...]
        for source in range(came_ref.shape[0]):
            total = total + came_ref[source, z]
        for rep in range(sum_ref.shape[0] // SIDE):
            sum_ref[rep * SIDE + z] = total


def finish(scale, part, came_ref, zero_ref, kernel_ref, bias_ref, gain_ref, shift_ref):
    total = zero_ref[...]
    for source in range(came_ref.shape[0]):
        total = total + came_ref[source]
    total = total * scale
    taps = kernel_ref.shape[0]
    kernel_ref[...] = total[:taps, :part]
    bias_ref[...] = total[taps : taps + 1, :part]
    for row, ref in ((0, gain_ref), (1, shift_ref)):
        ref[...] = jnp.concatenate(
            [total[SUB * c + row : SUB * c + row + 1, part:] for c in range(3)], axis=1
        )


ANY = pl.BlockSpec(memory_space=pl.ANY)
HELD = pl.BlockSpec(memory_space=pltpu.VMEM)


def run_first(x, cotangent, place, params, taps):
    frames, width = x.shape
    tiles = width // LANES
    chunks = 8
    rows = params.shape[1] // SIDE
    groups = (SIDE * SIDE, rows, SIDE * params.shape[2])
    padded = frames + 2 * PAD
    whole = (tiles, frames, LANES)
    return pl.pallas_call(
        functools.partial(forward_and_kernel_grad, taps),
        out_shape=(
            jax.ShapeDtypeStruct((frames, width), jnp.bfloat16),
            jax.ShapeDtypeStruct((tiles, padded, LANES), F32),
            jax.ShapeDtypeStruct((SIDE**3, MAIN, LANES), F32),
            jax.ShapeDtypeStruct(groups, params.dtype),
        ),
        in_specs=[pl.BlockSpec(memory_space=pltpu.SMEM), ANY, ANY, HELD],
        out_specs=(ANY, ANY, HELD, ANY),
        scratch_shapes=[
            pltpu.VMEM((frames, width), jnp.bfloat16),
            pltpu.VMEM((frames, width), jnp.bfloat16),
            pltpu.VMEM((frames, width), jnp.bfloat16),
            pltpu.VMEM((padded + SUB, LANES), F32),
            pltpu.VMEM((tiles, frames // 2 + 3 * SUB, LANES), F32),
            pltpu.VMEM((tiles, frames // 2 + 3 * SUB, LANES), F32),
            pltpu.VMEM((tiles, frames // 2 + 3 * SUB, LANES), F32),
            pltpu.VMEM((frames // 2, LANES), F32),
            pltpu.VMEM((frames // 2 + SUB, LANES), F32),
            pltpu.VMEM((frames // 2, LANES), F32),
            pltpu.VMEM(whole, F32),
            pltpu.VMEM(whole, F32),
            pltpu.VMEM((tiles, padded, LANES), F32),
            pltpu.VMEM((rows, LANES), F32),
            pltpu.VMEM((tiles, MAIN + SUB, LANES), F32),
            pltpu.VMEM((frames, LANES), F32),
            pltpu.VMEM((frames, LANES), F32),
            pltpu.VMEM((frames, LANES), F32),
            pltpu.VMEM((frames, LANES), F32),
            pltpu.VMEM(groups, params.dtype),
            pltpu.SemaphoreType.DMA((chunks,)),
            pltpu.SemaphoreType.DMA((chunks,)),
            pltpu.SemaphoreType.DMA((chunks,)),
            pltpu.SemaphoreType.DMA((chunks,)),
            pltpu.SemaphoreType.DMA,
        ],
        compiler_params=pltpu.CompilerParams(vmem_limit_bytes=52 << 20),
        cost_estimate=pl.CostEstimate(
            flops=4 * taps * frames * width, bytes_accessed=20 * frames * width, transcendentals=0
        ),
        name="forward_and_kernel_grad",
    )(place, x, cotangent, params)


def run_second(grad_conv, params, taps, frames, width, chunks, begun=None):
    tiles = width // LANES
    share = (chunks[1] - chunks[0]) * CHUNK_TILES / tiles
    count = tiles // CHUNK_TILES
    return pl.pallas_call(
        functools.partial(input_grad, taps, chunks),
        out_shape=(
            jax.ShapeDtypeStruct((frames, width), jnp.bfloat16),
            jax.ShapeDtypeStruct((MAIN, LANES), F32),
        ),
        in_specs=[ANY, HELD] + ([] if begun is None else [ANY]),
        out_specs=(ANY, HELD),
        scratch_shapes=[
            pltpu.VMEM(grad_conv.shape, F32),
            pltpu.VMEM((frames, width), jnp.bfloat16),
            pltpu.VMEM((params.shape[1], LANES), F32),
            pltpu.SemaphoreType.DMA((count,)),
            pltpu.SemaphoreType.DMA((count,)),
        ],
        input_output_aliases={} if begun is None else {2: 0},
        compiler_params=pltpu.CompilerParams(vmem_limit_bytes=52 << 20),
        cost_estimate=pl.CostEstimate(
            flops=int(2 * taps * frames * width * share),
            bytes_accessed=int(6 * frames * width * share),
            transcendentals=0,
        ),
        name="input_grad",
    )(grad_conv, params, *([] if begun is None else [begun]))


def small(body, out_shape, name, *operands, scalars=0):
    scalar = pl.BlockSpec(memory_space=pltpu.SMEM)
    many = isinstance(out_shape, tuple)
    return pl.pallas_call(
        body,
        out_shape=out_shape,
        in_specs=[scalar] * scalars + [HELD] * (len(operands) - scalars),
        out_specs=(HELD,) * len(out_shape) if many else HELD,
        compiler_params=pltpu.CompilerParams(vmem_limit_bytes=8 << 20),
        name=name,
    )(*operands)


def per_device(conv_input, cotangent, kernel, conv_bias, ln_gain, ln_bias):
    taps = kernel.shape[0]
    clips, frames, width = conv_input.shape
    packed = jnp.concatenate([kernel, conv_bias[None], ln_gain[None], ln_bias[None]], 0)
    packed = jnp.pad(packed, ((0, -packed.shape[0] % SUB), (0, 0)))
    params = gather_channels(packed)
    me = lax.axis_index("shard")
    place = (me // (SIDE * SIDE))[None]
    activated, grad_conv, pieces, groups = run_first(
        conv_input[0], cotangent[0], place, params, taps
    )
    part_of = functools.partial(run_second, grad_conv, groups, taps, frames, width)
    came = lax.all_to_all(
        pieces.reshape(SIDE * SIDE, SIDE, MAIN, LANES), "shard", 0, 0, axis_index_groups=plane_groups()
    )
    begun, zeros = part_of((0, EARLY))
    reps, plane = lax.axis_size("rep"), SIDE * SIDE
    shape = jax.ShapeDtypeStruct((reps * SIDE,) + zeros.shape, F32)
    sums = small(sum_plane, shape, "sum_plane", came, zeros)
    columns = [
        [rep * SIDE**3 + z * plane + at for rep in range(reps) for z in range(SIDE)]
        for at in range(plane)
    ]
    came = lax.all_to_all(sums, ("rep", "shard"), 0, 0, axis_index_groups=columns)
    grad_input, zeros = part_of((EARLY, width // LANES // CHUNK_TILES), begun)
    count = clips * frames * lax.axis_size("rep") * lax.axis_size("shard")
    part = kernel.shape[1]
    row = jax.ShapeDtypeStruct((1, part), F32)
    grads = small(
        functools.partial(finish, 1.0 / math.sqrt(count), part),
        (jax.ShapeDtypeStruct((taps, part), F32), row, row, row),
        "finish", came, zeros,
    )
    return (activated[None], grad_input[None], grads[0]) + tuple(g[0] for g in grads[1:])


def solution(mesh):
    data = P(("rep", "shard"), None, None)
    wide = P(None, "shard")
    narrow = P("shard")
    return jax.shard_map(
        per_device,
        mesh=mesh,
        in_specs=(data, data, wide, narrow, narrow, narrow),
        out_specs=(data, data, wide, narrow, narrow, narrow),
        check_vma=False,
    )
```

```python
import functools
import math

import jax
import jax.numpy as jnp
from jax import lax
from jax.experimental import pallas as pl
from jax.experimental.pallas import tpu as pltpu
from jax.sharding import PartitionSpec as P

SIDE = 4
LANES = 128
SUB = 8
PAD = 16
F32 = jnp.float32
CHUNK_TILES = 3
EARLY = 10
MAIN = 32


def shifted(axis_stride, step):
    pairs = []
    for source in range(SIDE**3):
        at = (source // axis_stride) % SIDE
        pairs.append((source, source + ((at + step) % SIDE - at) * axis_stride))
    return pairs


def plane_groups():
    plane = SIDE * SIDE
    return [list(range(z * plane, (z + 1) * plane)) for z in range(SIDE)]


def spread(*refs):
    out_ref = refs[-1]
    rows = refs[0].shape[0]
    for to in range(out_ref.shape[0]):
        for slot, ref in enumerate(refs[:-1]):
            out_ref[to, slot * rows : (slot + 1) * rows, :] = ref[...]


def gather_channels(packed):
    stride = SIDE * SIDE
    column = [packed] + [
        lax.ppermute(packed, "shard", shifted(stride, step)) for step in range(1, SIDE)
    ]
    shape = jax.ShapeDtypeStruct((stride, SIDE * packed.shape[0], packed.shape[1]), packed.dtype)
    same = small(spread, shape, "spread", *column)
    return lax.all_to_all(same, "shard", 0, 0, axis_index_groups=plane_groups())


def place_params(came, at_z, p_ref):
    rows = p_ref.shape[1]
    for y in range(SIDE):
        for slot in range(SIDE):
            group = lax.rem(at_z - slot + SIDE, SIDE) * SIDE + y
            at = slice(slot * rows, (slot + 1) * rows)
            p_ref[group] = jnp.concatenate(
                [came[y * SIDE + x, at, :] for x in range(SIDE)], axis=1
            )


def bcast_row(ref, row):
    return jnp.broadcast_to(ref[pl.ds(row, 1), :], (SUB, LANES))


def forward_and_kernel_grad(
    taps, at_ref, x_hbm, ct_hbm, came_ref, act_hbm, gc_hbm, gr_ref, p_hbm,
    xb, cb, ab, xs, xe, xo, xt, fa, fb, fc, cv, gn, gc, pf, st, s1, s2, row_a, row_b, p_ref, x_sem, c_sem, a_sem, g_sem, p_sem,
):
    frames, width = xb.shape
    tiles = width // LANES
    rows = frames // SUB
    chunks = x_sem.shape[0]
    per_chunk = tiles // chunks
    per_group = p_ref.shape[2] // LANES
    block = 8

    def lanes_of(tile):
        return pl.ds(pl.multiple_of(tile * LANES, LANES), LANES)

    def chunk_lanes(chunk):
        wide = per_chunk * LANES
        return pl.ds(pl.multiple_of(chunk * wide, wide), wide)

    def x_copy(chunk):
        return pltpu.make_async_copy(
            x_hbm.at[:, chunk_lanes(chunk)], xb.at[:, chunk_lanes(chunk)], x_sem.at[chunk]
        )

    def c_copy(chunk):
        return pltpu.make_async_copy(
            ct_hbm.at[:, chunk_lanes(chunk)], cb.at[:, chunk_lanes(chunk)], c_sem.at[chunk]
        )

    def a_copy(chunk):
        return pltpu.make_async_copy(
            ab.at[:, chunk_lanes(chunk)], act_hbm.at[:, chunk_lanes(chunk)], a_sem.at[chunk]
        )

    def g_copy(chunk):
        at = pl.ds(chunk * per_chunk, per_chunk)
        return pltpu.make_async_copy(gc.at[at], gc_hbm.at[at], g_sem.at[chunk])

    for chunk in range(chunks):
        x_copy(chunk).start()
    for chunk in range(chunks):
        c_copy(chunk).start()
    place_params(came_ref, at_ref[0], p_ref)
    p_copy = pltpu.make_async_copy(p_ref, p_hbm, p_sem)
    p_copy.start()
    st[...] = jnp.zeros_like(st)

    def load_params(tile):
        group = tile // per_group
        inside = tile - group * per_group
        lanes = pl.ds(pl.multiple_of(inside * LANES, LANES), LANES)
        pf[...] = p_ref[group, :, lanes].astype(F32)

    zero = jnp.zeros((SUB, LANES), F32)
    s1[...] = jnp.zeros_like(s1)
    s2[...] = jnp.zeros_like(s2)

    for edge in (0, SUB, PAD + frames, PAD + frames + SUB, PAD + frames + 2 * SUB):
        xs[pl.ds(edge, SUB), :] = zero

    def conv_tile(tile, _):
        load_params(tile)
        for edge in (0, SUB, PAD + frames, PAD + frames + SUB):
            gc[tile, pl.ds(edge, SUB), :] = zero
        xs[pl.ds(PAD, frames), :] = xb[:, lanes_of(tile)].astype(F32)
        half = rows // 2
        xo[tile, pl.ds(SUB * (half + 2), SUB), :] = zero
        for r in range(half + 2):
            at = pl.ds(SUB * r, SUB)
            even = xs[pl.ds(2 * SUB * r + 1, SUB, stride=2), :]
            odd = xs[pl.ds(2 * SUB * r + 2, SUB, stride=2), :]
            xe[tile, at, :] = even
            xo[tile, at, :] = odd
            xt[tile, at, :] = even + odd
        bias = bcast_row(pf, taps)

        def run(source, weights, first, count, start, store):
            for r0 in range(0, count, 16):
                size = min(16, count - r0)
                acc = [start] * size
                for phase in range(SUB):
                    depth = len(range(phase, len(weights), SUB))
                    for i in range(size + depth - 1):
                        value = source[tile, pl.ds(SUB * (r0 + i) + phase + first, SUB), :]
                        for q in range(depth):
                            if 0 <= i - q < size:
                                term = value * weights[phase + SUB * q]
                                before = acc[i - q]
                                acc[i - q] = term if before is None else before + term
                for b in range(size):
                    store(r0 + b, acc[b])

        w_even = [bcast_row(pf, 2 * e) for e in range(taps // 2 + 1)]
        w_odd = [bcast_row(pf, 2 * e + 1) for e in range(taps // 2)]

        def keep(ref):
            def store(r, value):
                ref[pl.ds(SUB * r, SUB), :] = value
            return store

        run(xo, w_odd, 0, half + 1, None, keep(fb))
        run(xe, w_even, 0, half, bias, keep(fa))
        w_both = [w_even[0]] + [w_even[e] + w_odd[e - 1] for e in range(1, len(w_even))]

        def last(r, value):
            here = pl.ds(SUB * r, SUB)
            own, before, after = fa[here, :], fb[here, :], fb[pl.ds(SUB * r + 1, SUB), :]
            even = own + before
            odd = (value - own) - after + (bias + bias)
            cv[tile, pl.ds(2 * SUB * r, SUB, stride=2), :] = even
            cv[tile, pl.ds(2 * SUB * r + 1, SUB, stride=2), :] = odd
            s2[here, :] += even
            s2[pl.ds(SUB * (half + r), SUB), :] += odd

        run(xt, w_both, 0, half, None, last)
        return 0

    def conv_chunk(chunk, _):
        x_copy(chunk).wait()
        lax.fori_loop(chunk * per_chunk, (chunk + 1) * per_chunk, conv_tile, 0)
        return 0

    lax.fori_loop(0, chunks, conv_chunk, 0)
    for r in range(rows // 2):
        here = pl.ds(SUB * r, SUB)
        s1[pl.ds(2 * SUB * r, SUB, stride=2), :] = s2[here, :]
        s1[pl.ds(2 * SUB * r + 1, SUB, stride=2), :] = s2[pl.ds(frames // 2 + SUB * r, SUB), :]
    s2[...] = jnp.zeros_like(s2)

    row_a[...] = jnp.broadcast_to(
        jnp.sum(s1[...], axis=1, keepdims=True) * (1.0 / width), s1.shape
    )

    def var_tile(tile, _):
        for r in range(rows):
            at = pl.ds(SUB * r, SUB)
            off = cv[tile, at, :] - row_a[at, :]
            s2[at, :] += off * off
        return 0

    lax.fori_loop(0, tiles, var_tile, 0)
    row_b[...] = jnp.broadcast_to(
        lax.rsqrt(jnp.sum(s2[...], axis=1, keepdims=True) * (1.0 / width) + 1e-05), s2.shape
    )
    s1[...] = jnp.zeros_like(s1)
    s2[...] = jnp.zeros_like(s2)

    def act_tile(tile, _):
        load_params(tile)
        gain = bcast_row(pf, taps + 1)
        shift = bcast_row(pf, taps + 2)
        sum_gain, sum_shift = zero, zero
        for r0 in range(0, rows, 4):
            outs = []
            span = pl.ds(SUB * r0, SUB * 4)
            upstream = cb[span, lanes_of(tile)].astype(F32)
            for b in range(4):
                at = pl.ds(SUB * (r0 + b), SUB)
                normed = (cv[tile, at, :] - row_a[at, :]) * row_b[at, :]
                affine = gain * normed + shift
                squash = 0.5 * jnp.tanh(0.5 * affine) + 0.5
                act = affine * squash
                outs.append(act)
                ga = upstream[SUB * b : SUB * (b + 1)] * (squash * (1.0 + (affine - act)))
                sum_gain = sum_gain + ga * normed
                sum_shift = sum_shift + ga
                scaled = ga * gain
                cv[tile, at, :] = normed
                gn[tile, at, :] = scaled
                s1[at, :] += scaled
                s2[at, :] += scaled * normed
            ab[span, lanes_of(tile)] = jnp.concatenate(outs, 0).astype(ab.dtype)
        st[tile, pl.ds(taps + 1, 1), :] = jnp.sum(sum_gain, axis=0, keepdims=True)
        st[tile, pl.ds(taps + 2, 1), :] = jnp.sum(sum_shift, axis=0, keepdims=True)
        return 0

    def act_chunk(chunk, _):
        c_copy(chunk).wait()
        lax.fori_loop(chunk * per_chunk, (chunk + 1) * per_chunk, act_tile, 0)
        a_copy(chunk).start()
        return 0

    lax.fori_loop(0, chunks, act_chunk, 0)

    mean_gn = jnp.sum(s1[...], axis=1, keepdims=True) * (1.0 / width)
    mean_gnn = jnp.sum(s2[...], axis=1, keepdims=True) * (1.0 / width)
    s1[...] = jnp.broadcast_to(mean_gn, s1.shape)
    s2[...] = jnp.broadcast_to(mean_gnn, s2.shape)

    def grad_tile(tile, _):
        total = zero
        for r0 in range(0, rows, block):
            for b in range(block):
                at = pl.ds(SUB * (r0 + b), SUB)
                grad = row_b[at, :] * (
                    gn[tile, at, :] - s1[at, :] - cv[tile, at, :] * s2[at, :]
                )
                gc[tile, pl.ds(PAD + SUB * (r0 + b), SUB), :] = grad
                total = total + grad
        half = rows // 2
        for r in range(half):
            here = pl.ds(SUB * r, SUB)
            g_even = gc[tile, pl.ds(PAD + 2 * SUB * r, SUB, stride=2), :]
            g_odd = gc[tile, pl.ds(PAD + 2 * SUB * r + 1, SUB, stride=2), :]
            fa[here, :] = g_even - g_odd
            fc[here, :] = g_odd
        for r in range(half + 1):
            g_even = gc[tile, pl.ds(PAD + 2 * SUB * r, SUB, stride=2), :]
            g_before = gc[tile, pl.ds(PAD + 2 * SUB * r - 1, SUB, stride=2), :]
            fb[pl.ds(SUB * r, SUB), :] = g_even - g_before

        def corr(source, grads, count, size):
            acc = [zero] * size
            for r0 in range(0, count, block):
                many = min(block, count - r0)
                held = [grads[pl.ds(SUB * (r0 + b), SUB), :] for b in range(many)]
                for phase in range(SUB):
                    depth = len(range(phase, size, SUB))
                    for i in range(many + depth - 1):
                        value = source[tile, pl.ds(SUB * (r0 + i) + phase, SUB), :]
                        for q in range(depth):
                            if 0 <= i - q < many:
                                acc[phase + SUB * q] = acc[phase + SUB * q] + value * held[i - q]
            return acc

        d_even = corr(xe, fa, half, taps // 2 + 1)
        d_both = corr(xt, fc, half, taps // 2 + 1)
        for e in range(taps // 2 + 1):
            st[tile, pl.ds(2 * e, 1), :] = jnp.sum(d_even[e] + d_both[e], axis=0, keepdims=True)
        d_odd = corr(xo, fb, half + 1, taps // 2)
        for e in range(taps // 2):
            both = d_odd[e] + d_both[e + 1]
            st[tile, pl.ds(2 * e + 1, 1), :] = jnp.sum(both, axis=0, keepdims=True)
        st[tile, pl.ds(taps, 1), :] = jnp.sum(total, axis=0, keepdims=True)
        return 0

    def grad_chunk(chunk, _):
        lax.fori_loop(chunk * per_chunk, (chunk + 1) * per_chunk, grad_tile, 0)
        g_copy(chunk).start()
        return 0

    lax.fori_loop(0, chunks, grad_chunk, 0)

    def out_group(group, _):
        whole = jnp.concatenate(
            [st[group * per_group + u, :, :] for u in range(per_group)], axis=1
        )
        part = per_group * LANES // SIDE
        for a in range(SIDE):
            piece = whole[:, a * part : (a + 1) * part]
            spill = piece[MAIN : MAIN + SUB]
            width_left = LANES - part
            side = [spill[:, c : c + width_left] for c in range(0, part, width_left)]
            side.append(jnp.zeros((SUB, width_left), F32))
            both = jnp.concatenate([piece[:MAIN], jnp.concatenate(side, 0)], axis=1)
            at_yx = lax.rem(group, SIDE) * SIDE + a
            gr_ref[at_yx * SIDE + group // SIDE] = both
        return 0

    lax.fori_loop(0, tiles // per_group, out_group, 0)
    for chunk in range(chunks):
        a_copy(chunk).wait()
        g_copy(chunk).wait()
    p_copy.wait()


def input_grad(taps, chunks, gc_hbm, p_ref, *refs):
    gi_hbm, zero_ref, gc, gb, pf, g_sem, o_sem = refs[-7:]
    rows = gb.shape[0] // SUB
    per_chunk = CHUNK_TILES
    per_group = p_ref.shape[2] // LANES
    block = 8

    def g_copy(chunk):
        at = pl.ds(chunk * per_chunk, per_chunk)
        return pltpu.make_async_copy(gc_hbm.at[at], gc.at[at], g_sem.at[chunk])

    def o_copy(chunk):
        wide = per_chunk * LANES
        at = pl.ds(pl.multiple_of(chunk * wide, wide), wide)
        return pltpu.make_async_copy(gb.at[:, at], gi_hbm.at[:, at], o_sem.at[chunk])

    for chunk in range(*chunks):
        g_copy(chunk).start()
    zero_ref[...] = jnp.zeros_like(zero_ref)

    def tile_step(tile, _):
        group = tile // per_group
        inside = tile - group * per_group
        lanes = pl.ds(pl.multiple_of(inside * LANES, LANES), LANES)
        pf[...] = p_ref[group, :, lanes].astype(F32)
        weights = [bcast_row(pf, taps - 1 - j) for j in range(taps)]
        for r0 in range(0, rows, block):
            acc = [None] * block
            for phase in range(SUB):
                depth = len(range(phase, taps, SUB))
                for i in range(block + depth - 1):
                    value = gc[tile, pl.ds(SUB * (r0 + i) + phase + 1, SUB), :]
                    for q in range(depth):
                        b = i - q
                        if 0 <= b < block:
                            term = value * weights[phase + SUB * q]
                            acc[b] = term if acc[b] is None else acc[b] + term
            at = pl.ds(pl.multiple_of(tile * LANES, LANES), LANES)
            gb[pl.ds(SUB * r0, SUB * block), at] = jnp.concatenate(acc, 0).astype(gb.dtype)
        return 0

    def chunk_step(chunk, _):
        g_copy(chunk).wait()
        lax.fori_loop(chunk * per_chunk, (chunk + 1) * per_chunk, tile_step, 0)
        o_copy(chunk).start()
        return 0

    lax.fori_loop(*chunks, chunk_step, 0)
    for chunk in range(*chunks):
        o_copy(chunk).wait()


def sum_plane(came_ref, zero_ref, sum_ref):
    for z in range(SIDE):
        total = zero_ref[...]
        for source in range(came_ref.shape[0]):
            total = total + came_ref[source, z]
        for rep in range(sum_ref.shape[0] // SIDE):
            sum_ref[rep * SIDE + z] = total


def finish(scale, part, came_ref, zero_ref, kernel_ref, bias_ref, gain_ref, shift_ref):
    total = zero_ref[...]
    for source in range(came_ref.shape[0]):
        total = total + came_ref[source]
    total = total * scale
    taps = kernel_ref.shape[0]
    kernel_ref[...] = total[:taps, :part]
    bias_ref[...] = total[taps : taps + 1, :part]
    for row, ref in ((0, gain_ref), (1, shift_ref)):
        ref[...] = jnp.concatenate(
            [total[SUB * c + row : SUB * c + row + 1, part:] for c in range(3)], axis=1
        )


ANY = pl.BlockSpec(memory_space=pl.ANY)
HELD = pl.BlockSpec(memory_space=pltpu.VMEM)


def run_first(x, cotangent, place, params, taps):
    frames, width = x.shape
    tiles = width // LANES
    chunks = 8
    rows = params.shape[1] // SIDE
    groups = (SIDE * SIDE, rows, SIDE * params.shape[2])
    padded = frames + 2 * PAD
    whole = (tiles, frames, LANES)
    return pl.pallas_call(
        functools.partial(forward_and_kernel_grad, taps),
        out_shape=(
            jax.ShapeDtypeStruct((frames, width), jnp.bfloat16),
            jax.ShapeDtypeStruct((tiles, padded, LANES), F32),
            jax.ShapeDtypeStruct((SIDE**3, MAIN, LANES), F32),
            jax.ShapeDtypeStruct(groups, params.dtype),
        ),
        in_specs=[pl.BlockSpec(memory_space=pltpu.SMEM), ANY, ANY, HELD],
        out_specs=(ANY, ANY, HELD, ANY),
        scratch_shapes=[
            pltpu.VMEM((frames, width), jnp.bfloat16),
            pltpu.VMEM((frames, width), jnp.bfloat16),
            pltpu.VMEM((frames, width), jnp.bfloat16),
            pltpu.VMEM((padded + SUB, LANES), F32),
            pltpu.VMEM((tiles, frames // 2 + 3 * SUB, LANES), F32),
            pltpu.VMEM((tiles, frames // 2 + 3 * SUB, LANES), F32),
            pltpu.VMEM((tiles, frames // 2 + 3 * SUB, LANES), F32),
            pltpu.VMEM((frames // 2, LANES), F32),
            pltpu.VMEM((frames // 2 + SUB, LANES), F32),
            pltpu.VMEM((frames // 2, LANES), F32),
            pltpu.VMEM(whole, F32),
            pltpu.VMEM(whole, F32),
            pltpu.VMEM((tiles, padded, LANES), F32),
            pltpu.VMEM((rows, LANES), F32),
            pltpu.VMEM((tiles, MAIN + SUB, LANES), F32),
            pltpu.VMEM((frames, LANES), F32),
            pltpu.VMEM((frames, LANES), F32),
            pltpu.VMEM((frames, LANES), F32),
            pltpu.VMEM((frames, LANES), F32),
            pltpu.VMEM(groups, params.dtype),
            pltpu.SemaphoreType.DMA((chunks,)),
            pltpu.SemaphoreType.DMA((chunks,)),
            pltpu.SemaphoreType.DMA((chunks,)),
            pltpu.SemaphoreType.DMA((chunks,)),
            pltpu.SemaphoreType.DMA,
        ],
        compiler_params=pltpu.CompilerParams(vmem_limit_bytes=52 << 20),
        cost_estimate=pl.CostEstimate(
            flops=4 * taps * frames * width, bytes_accessed=20 * frames * width, transcendentals=0
        ),
        name="forward_and_kernel_grad",
    )(place, x, cotangent, params)


def run_second(grad_conv, params, taps, frames, width, chunks, begun=None):
    tiles = width // LANES
    share = (chunks[1] - chunks[0]) * CHUNK_TILES / tiles
    count = tiles // CHUNK_TILES
    return pl.pallas_call(
        functools.partial(input_grad, taps, chunks),
        out_shape=(
            jax.ShapeDtypeStruct((frames, width), jnp.bfloat16),
            jax.ShapeDtypeStruct((MAIN, LANES), F32),
        ),
        in_specs=[ANY, HELD] + ([] if begun is None else [ANY]),
        out_specs=(ANY, HELD),
        scratch_shapes=[
            pltpu.VMEM(grad_conv.shape, F32),
            pltpu.VMEM((frames, width), jnp.bfloat16),
            pltpu.VMEM((params.shape[1], LANES), F32),
            pltpu.SemaphoreType.DMA((count,)),
            pltpu.SemaphoreType.DMA((count,)),
        ],
        input_output_aliases={} if begun is None else {2: 0},
        compiler_params=pltpu.CompilerParams(vmem_limit_bytes=52 << 20),
        cost_estimate=pl.CostEstimate(
            flops=int(2 * taps * frames * width * share),
            bytes_accessed=int(6 * frames * width * share),
            transcendentals=0,
        ),
        name="input_grad",
    )(grad_conv, params, *([] if begun is None else [begun]))


def small(body, out_shape, name, *operands, scalars=0):
    scalar = pl.BlockSpec(memory_space=pltpu.SMEM)
    many = isinstance(out_shape, tuple)
    return pl.pallas_call(
        body,
        out_shape=out_shape,
        in_specs=[scalar] * scalars + [HELD] * (len(operands) - scalars),
        out_specs=(HELD,) * len(out_shape) if many else HELD,
        compiler_params=pltpu.CompilerParams(vmem_limit_bytes=8 << 20),
        name=name,
    )(*operands)


def per_device(conv_input, cotangent, kernel, conv_bias, ln_gain, ln_bias):
    taps = kernel.shape[0]
    clips, frames, width = conv_input.shape
    packed = jnp.concatenate([kernel, conv_bias[None], ln_gain[None], ln_bias[None]], 0)
    packed = jnp.pad(packed, ((0, -packed.shape[0] % SUB), (0, 0)))
    params = gather_channels(packed)
    me = lax.axis_index("shard")
    place = (me // (SIDE * SIDE))[None]
    activated, grad_conv, pieces, groups = run_first(
        conv_input[0], cotangent[0], place, params, taps
    )
    part_of = functools.partial(run_second, grad_conv, groups, taps, frames, width)
    came = lax.all_to_all(
        pieces.reshape(SIDE * SIDE, SIDE, MAIN, LANES), "shard", 0, 0, axis_index_groups=plane_groups()
    )
    begun, zeros = part_of((0, EARLY))
    reps, plane = lax.axis_size("rep"), SIDE * SIDE
    shape = jax.ShapeDtypeStruct((reps * SIDE,) + zeros.shape, F32)
    sums = small(sum_plane, shape, "sum_plane", came, zeros)
    columns = [
        [rep * SIDE**3 + z * plane + at for rep in range(reps) for z in range(SIDE)]
        for at in range(plane)
    ]
    came = lax.all_to_all(sums, ("rep", "shard"), 0, 0, axis_index_groups=columns)
    grad_input, zeros = part_of((EARLY, width // LANES // CHUNK_TILES), begun)
    count = clips * frames * lax.axis_size("rep") * lax.axis_size("shard")
    part = kernel.shape[1]
    row = jax.ShapeDtypeStruct((1, part), F32)
    grads = small(
        functools.partial(finish, 1.0 / math.sqrt(count), part),
        (jax.ShapeDtypeStruct((taps, part), F32), row, row, row),
        "finish", came, zeros,
    )
    return (activated[None], grad_input[None], grads[0]) + tuple(g[0] for g in grads[1:])


def solution(mesh):
    data = P(("rep", "shard"), None, None)
    wide = P(None, "shard")
    narrow = P("shard")
    return jax.shard_map(
        per_device,
        mesh=mesh,
        in_specs=(data, data, wide, narrow, narrow, narrow),
        out_specs=(data, data, wide, narrow, narrow, narrow),
        check_vma=False,
    )
```
